32 devices in a mesh: rep: 2 (over x), seq: 8 (over z, core), chan: 2 (over y).
Axes of the slice: x: 2, y: 2, z: 4, core: 2. Of those that a mesh axis runs over, the one named last changes fastest.
Arguments:
- inputs: bfloat16 [2, 8192, 256], P('rep', 'seq', 'chan'), may hold values from -6 to 6
- cotangent: bfloat16 [2, 8192, 256], P('rep', 'seq', 'chan'), may hold values from -0.046875 to 0.046875
- filter_taps: bfloat16 [8192, 256], P('seq', 'chan'), may hold values from -6 to 6
- out_proj: bfloat16 [256, 256], P('chan'), may hold values from -0.375 to 0.375
Outputs:
- grad_input: bfloat16 [2, 8192, 256], P('rep', 'seq', 'chan')
- grad_filter: float32 [8192, 256], P('seq', 'chan')
The draws below stay inside these ranges and needn't reach their ends.
All inputs are finite; a program needn't handle non-finite values.
Results may differ from the reference program's by a relative error of at most 0.0049.
Values may be sent and summed in bfloat16 or wider, within the bound.
No kernel may reach another device: no remote copies, remote signals or barrier semaphores. Data moves between devices by JAX's collectives and lax.ppermute only.
A program may use at most 128 MiB of HBM per device.

```python
import jax
import jax.numpy as jnp

C = 256
LENGTH = 8192
SEQS = 2


def level_of(key, shape, split, smallest, largest):
    level = 1.0
    for axis_at, parts in split:
        steps = jax.random.uniform(jax.random.fold_in(jax.random.fold_in(key, 6), axis_at), (parts,), jnp.float32, smallest / len(split), largest / len(split))
        level = level * jnp.repeat(jnp.exp(steps), shape[axis_at] // parts).reshape((-1,) + (1,) * (len(shape) - 1 - axis_at))
    return level


def bell_draw(stream_key, shape, deviation, limit, cuts=(), held_as=jnp.bfloat16):
    entries = jax.random.normal(stream_key, shape, jnp.float32) * deviation
    if len(cuts) > 0:
        entries = level_of(stream_key, shape, cuts, -0.22, 0.18) * entries
    return jnp.clip(entries, min=-limit, max=limit).astype(held_as)


def setup_inputs(seed: int = 0) -> dict:
    keys = jax.random.split(jax.random.key(seed), 5)
    return {
        "inputs": bell_draw(keys[0], (SEQS, LENGTH, C), 1.0, 6.0, ((0, 2), (1, 8), (2, 2))),
        "cotangent": bell_draw(keys[1], (SEQS, LENGTH, C), ((2 * LENGTH) ** -0.5), 0.046875, ((0, 2), (1, 8), (2, 2))),
        "filter_taps": bell_draw(keys[2], (LENGTH, C), 1.0, 6.0, ((0, 8), (1, 2))),
        "out_proj": bell_draw(keys[3], (C, C), C ** -0.5, 0.375, ((0, 2),)),
    }


def reference(inputs, cotangent, filter_taps, out_proj):
    extent = 2 * LENGTH
    grad_mixed = jnp.dot(cotangent.reshape(SEQS * LENGTH, C), out_proj.T, preferred_element_type=jnp.float32)
    grad_mixed = grad_mixed.astype(jnp.bfloat16).reshape(SEQS, LENGTH, C)
    width_block = min(256, C)
    input_cols = []
    filter_cols = []
    for col_start in range(0, C, width_block):
        col_end = col_start + width_block
        filter_spec = jnp.fft.fft(filter_taps[:, col_start:col_end].astype(jnp.float32), n=extent, axis=0)
        grad_list = []
        spec_sum = None
        for member in range(SEQS):
            grad_spec = jnp.fft.fft(grad_mixed[member, :, col_start:col_end].astype(jnp.float32), n=extent, axis=0)
            input_spec = jnp.fft.fft(inputs[member, :, col_start:col_end].astype(jnp.float32), n=extent, axis=0)
            grad_list.append(jnp.fft.ifft(grad_spec * jnp.conj(filter_spec), axis=0)[:LENGTH].real.astype(jnp.bfloat16))
            spec_term = grad_spec * jnp.conj(input_spec)
            spec_sum = spec_term if spec_sum is None else spec_sum + spec_term
        input_cols.append(jnp.stack(grad_list))
        filter_cols.append(jnp.fft.ifft(spec_sum, axis=0)[:LENGTH].real.astype(jnp.float32))
    return jnp.concatenate(input_cols, axis=2), jnp.concatenate(filter_cols, axis=1)
```

```python
import math

import jax
import jax.numpy as jnp
import numpy as np
from jax import lax
from jax.experimental import pallas as pl
from jax.experimental.pallas import tpu as pltpu
from jax.sharding import PartitionSpec as P

LANES = 128
F32 = jnp.float32
BF16 = jnp.bfloat16
VMEM_LIMIT = 48 * 1024 * 1024


def split(values):
    high = values.astype(BF16)
    low = (values - high.astype(F32)).astype(BF16)
    return high, low


def split_table(table):
    table = np.asarray(table, np.float32)
    high = table.astype(BF16)
    low = (table - high.astype(np.float32)).astype(BF16)
    return np.stack([high, low])


def phase(numerator, modulus):
    angle = 2.0 * math.pi * np.mod(numerator, modulus) / modulus
    return np.cos(angle), np.sin(angle)


def tables(devices, groups, narrow, tok_rows):
    length = devices * tok_rows
    tiles = tok_rows // LANES
    rows = groups * devices * narrow
    dev = np.arange(devices)
    quarter = 4 * dev + 1
    cos_d, sin_d = phase(quarter[:, None] * dev[None, :], 4 * devices)
    eye_g, eye_c = np.eye(groups), np.eye(narrow)

    def expand(square):
        return np.einsum("gh,jd,ce->gjchde", eye_g, square, eye_c).reshape(rows, rows)

    cos_d, sin_d = expand(cos_d), expand(sin_d)
    first = split_table(np.concatenate([cos_d, -sin_d], axis=0))
    last = split_table(np.concatenate([cos_d.T, -sin_d.T], axis=1) / length)
    local = np.arange(tok_rows)
    cos_r, sin_r = phase(quarter[:, None] * local[None, :], 4 * length)

    def widen(block):
        block = np.broadcast_to(block[None, :, None, :], (groups, devices, narrow, tok_rows))
        return block.reshape(rows, tok_rows)

    turn = np.stack([widen(cos_r), widen(sin_r)]).astype(np.float32)
    lane = np.arange(LANES)
    step = np.arange(tiles)
    cos_s, sin_s = phase(step[:, None] * lane[None, :], tok_rows)
    small = np.stack([cos_s, sin_s]).astype(np.float32)
    cos_b, sin_b = phase(lane[:, None] * lane[None, :], LANES)
    forward = split_table(np.block([[cos_b, -sin_b], [sin_b, cos_b]]))
    inverse = split_table(np.block([[cos_b, sin_b], [-sin_b, cos_b]]))
    return first, last, turn, small, forward, inverse


def butterflies(real_parts, imag_parts, sign):
    size = len(real_parts)
    if size == 1:
        return real_parts, imag_parts
    even_re, even_im = butterflies(real_parts[0::2], imag_parts[0::2], sign)
    odd_re, odd_im = butterflies(real_parts[1::2], imag_parts[1::2], sign)
    low_re, low_im, high_re, high_im = [], [], [], []
    for index in range(size // 2):
        re, im = odd_re[index], odd_im[index]
        if index == 0:
            turned = (re, im)
        elif 4 * index == size:
            turned = (-im, re) if sign > 0 else (im, -re)
        else:
            angle = sign * 2.0 * math.pi * index / size
            c, s = math.cos(angle), math.sin(angle)
            if 8 * index == size:
                turned = ((re - im) * c, (re + im) * c) if sign > 0 else ((re + im) * c, (im - re) * c)
            else:
                turned = (re * c - im * s, re * s + im * c)
        low_re.append(even_re[index] + turned[0])
        low_im.append(even_im[index] + turned[1])
        high_re.append(even_re[index] - turned[0])
        high_im.append(even_im[index] - turned[1])
    return low_re + high_re, low_im + high_im


def dot(lhs, rhs):
    return jnp.dot(lhs, rhs, preferred_element_type=F32)


CHUNK = 16


def transform(block, first, turn, small, forward, stage, high, low, spectrum, rows, all_rows):
    tiles = block.shape[1] // LANES
    if rows == all_rows:
        stage[...] = dot(first[0], block) + dot(first[1], block)
    else:
        for part in range(2):
            pick = pl.ds(part * all_rows, rows)
            stage[part * rows : (part + 1) * rows, :] = dot(first[0, pick, :rows], block) + dot(
                first[1, pick, :rows], block
            )

    def body(index, carry):
        start = pl.multiple_of(index * CHUNK, CHUNK)
        res, ims = [], []
        for tile in range(tiles):
            lanes = pl.ds(tile * LANES, LANES)
            re = stage[pl.ds(start, CHUNK), lanes]
            im = stage[pl.ds(rows + start, CHUNK), lanes]
            c = turn[0, pl.ds(start, CHUNK), lanes]
            s = turn[1, pl.ds(start, CHUNK), lanes]
            res.append(re * c + im * s)
            ims.append(im * c - re * s)
        res, ims = butterflies(res, ims, -1.0)
        for tile in range(tiles):
            re, im = res[tile], ims[tile]
            if tile > 0:
                c, s = small[0, tile : tile + 1, :], small[1, tile : tile + 1, :]
                re, im = re * c + im * s, im * c - re * s
            at = pl.ds(tile * rows + start, CHUNK)
            for part, lanes in ((re, pl.ds(0, LANES)), (im, pl.ds(LANES, LANES))):
                part_high, part_low = split(part)
                high[at, lanes] = part_high
                low[at, lanes] = part_low
        return carry

    lax.fori_loop(0, rows // CHUNK, body, 0)
    count = tiles * rows
    wide = high[:count, :]
    spectrum[...] = dot(wide, forward[0]) + (dot(wide, forward[1]) + dot(low[:count, :], forward[0]))


def untransform(last, turn, small, inverse, stage, high, low, back_high, back_low, rows, all_rows, tiles):
    count = tiles * rows
    wide = high[:count, :]
    stage[:count, :] = dot(wide, inverse[0]) + (dot(wide, inverse[1]) + dot(low[:count, :], inverse[0]))

    def body(index, carry):
        start = pl.multiple_of(index * CHUNK, CHUNK)
        res, ims = [], []
        for tile in range(tiles):
            at = pl.ds(tile * rows + start, CHUNK)
            re = stage[at, pl.ds(0, LANES)]
            im = stage[at, pl.ds(LANES, LANES)]
            if tile > 0:
                c, s = small[0, tile : tile + 1, :], small[1, tile : tile + 1, :]
                re, im = re * c - im * s, im * c + re * s
            res.append(re)
            ims.append(im)
        res, ims = butterflies(res, ims, 1.0)
        for tile in range(tiles):
            lanes = pl.ds(tile * LANES, LANES)
            c = turn[0, pl.ds(start, CHUNK), lanes]
            s = turn[1, pl.ds(start, CHUNK), lanes]
            re, im = res[tile], ims[tile]
            for part, at in ((re * c - im * s, start), (im * c + re * s, rows + start)):
                part_high, part_low = split(part)
                back_high[pl.ds(at, CHUNK), lanes] = part_high
                back_low[pl.ds(at, CHUNK), lanes] = part_low
        return carry

    lax.fori_loop(0, rows // CHUNK, body, 0)
    if rows == all_rows:
        table_high, table_low = last[0], last[1]
    else:
        table_high, table_low = (
            jnp.concatenate([last[k, :rows, :rows], last[k, :rows, all_rows : all_rows + rows]], axis=1)
            for k in range(2)
        )
    right = back_high[: 2 * rows, :]
    return dot(table_high, right) + (dot(table_low, right) + dot(table_high, back_low[: 2 * rows, :]))


def identity(size, dtype):
    row = lax.broadcasted_iota(jnp.int32, (size, size), 0)
    col = lax.broadcasted_iota(jnp.int32, (size, size), 1)
    return (row == col).astype(dtype)


def flipped(left, right):
    return lax.dot_general(left, right, (((1,), (1,)), ((), ())), preferred_element_type=F32)


def per_device(inputs, cotangent, filter_taps, out_proj):
    devices = lax.axis_size("seq")
    groups = lax.axis_size("rep")
    chans = lax.axis_size("chan")
    tok_rows, chan_width = inputs.shape[1:]
    tiles = tok_rows // LANES
    narrow = chan_width // (groups * devices)
    peers = groups * devices
    rows = chan_width
    taps_rows = rows // groups
    part_rows = tok_rows // groups
    first, last, turn, small, forward, inverse = (
        jnp.asarray(t) for t in tables(devices, groups, narrow, tok_rows)
    )

    def call(kernel, out_shape, scratch=(), flops=10**8):
        return pl.pallas_call(
            kernel,
            out_shape=out_shape,
            scratch_shapes=scratch,
            compiler_params=pltpu.CompilerParams(vmem_limit_bytes=VMEM_LIMIT),
            cost_estimate=pl.CostEstimate(flops=flops, bytes_accessed=10**6, transcendentals=0),
        )

    def pack_kernel(input_ref, taps_ref, out_ref):
        eye = identity(chan_width, BF16)
        moved = flipped(eye, input_ref[...])
        out_ref[:, :, :tok_rows] = moved.reshape(peers, narrow, tok_rows).astype(BF16)
        start = pl.multiple_of(lax.axis_index("rep") * part_rows, part_rows)
        moved = flipped(eye, taps_ref[pl.ds(start, part_rows), :])
        out_ref[:, :, tok_rows:] = moved.reshape(peers, narrow, part_rows).astype(BF16)

    def mix_kernel(own_ref, other_ref, proj_ref, out_ref):
        chan = lax.axis_index("chan")
        own = pl.ds(pl.multiple_of(chan * chan_width, chan_width), chan_width)
        other = pl.ds(pl.multiple_of((1 - chan) * chan_width, chan_width), chan_width)
        mixed = flipped(proj_ref[:, own], own_ref[...]) + flipped(proj_ref[:, other], other_ref[...])
        out_ref[...] = mixed.reshape(peers, narrow, tok_rows).astype(BF16)

    def early_kernel(recv_ref, first, turn, small, forward, input_ref, taps_ref, stage, high, low):
        block = recv_ref[:, :, :tok_rows].astype(F32).reshape(rows, tok_rows).astype(BF16)
        transform(block, first, turn, small, forward, stage, high, low, input_ref, rows, rows)
        half = recv_ref[:, :, tok_rows:].astype(F32).reshape(groups, taps_rows, part_rows).astype(BF16)
        block = jnp.concatenate([half[k] for k in range(groups)], axis=1)
        transform(block, first, turn, small, forward, stage, high, low, taps_ref, taps_rows, rows)

    def late_kernel(
        recv_ref, input_ref, taps_ref, first, last, turn, small, forward, inverse,
        out_ref, stage, high, low, grad, back, back_high, back_low,
    ):
        block = recv_ref[...].astype(F32).reshape(rows, tok_rows).astype(BF16)
        transform(block, first, turn, small, forward, stage, high, low, grad, rows, rows)
        real, imag = pl.ds(0, LANES), pl.ds(LANES, LANES)

        def product(tile, carry):
            for group in range(groups):
                at = pl.ds(pl.multiple_of(tile * rows + group * taps_rows, taps_rows), taps_rows)
                tap = pl.ds(pl.multiple_of(tile * taps_rows, taps_rows), taps_rows)
                gr, gi = grad[at, real], grad[at, imag]
                kr, ki = taps_ref[tap, real], taps_ref[tap, imag]
                for part, lanes in ((gr * kr + gi * ki, real), (gi * kr - gr * ki, imag)):
                    part_high, part_low = split(part)
                    high[at, lanes] = part_high
                    low[at, lanes] = part_low
            return carry

        lax.fori_loop(0, tiles, product, 0)
        value = untransform(
            last, turn, small, inverse, back, high, low, back_high, back_low, rows, rows, tiles
        )
        out_ref[:, :, :tok_rows] = value.reshape(peers, narrow, tok_rows).astype(BF16)

        def summed(tile, carry):
            tap = pl.ds(pl.multiple_of(tile * taps_rows, taps_rows), taps_rows)
            re = im = None
            for group in range(groups):
                at = pl.ds(pl.multiple_of(tile * rows + group * taps_rows, taps_rows), taps_rows)
                gr, gi = grad[at, real], grad[at, imag]
                ur, ui = input_ref[at, real], input_ref[at, imag]
                term_re, term_im = gr * ur + gi * ui, gi * ur - gr * ui
                re = term_re if re is None else re + term_re
                im = term_im if im is None else im + term_im
            for part, lanes in ((re, real), (im, imag)):
                part_high, part_low = split(part)
                high[tap, lanes] = part_high
                low[tap, lanes] = part_low
            return carry

        lax.fori_loop(0, tiles, summed, 0)
        value = untransform(
            last, turn, small, inverse, back, high, low, back_high, back_low, taps_rows, rows, tiles
        )
        value = value.reshape(devices, narrow, tok_rows).astype(BF16)
        for group in range(groups):
            out_ref[group * devices : (group + 1) * devices, :, tok_rows:] = value

    def final_kernel(recv_ref, input_ref, taps_ref):
        eye = identity(chan_width, BF16)
        value = recv_ref[...].astype(F32).reshape(rows, 2 * tok_rows).astype(BF16)
        contract = (((0,), (0,)), ((), ()))
        moved = lax.dot_general(value[:, :tok_rows], eye, contract, preferred_element_type=F32)
        input_ref[...] = moved.astype(BF16)
        taps_ref[...] = lax.dot_general(value[:, tok_rows:], eye, contract, preferred_element_type=F32)

    def exchange(block):
        return lax.all_to_all(block, ("rep", "seq"), split_axis=0, concat_axis=0, tiled=True)

    shape = jax.ShapeDtypeStruct
    own = cotangent.reshape(tok_rows, chan_width)
    other = lax.ppermute(own, "chan", [(k, (k + 1) % chans) for k in range(chans)])
    sent = call(pack_kernel, shape((peers, narrow, tok_rows + part_rows), BF16))(
        inputs.reshape(tok_rows, chan_width), filter_taps
    )
    early = exchange(sent)
    mixed = call(mix_kernel, shape((peers, narrow, tok_rows), BF16))(own, other, out_proj)
    late = exchange(mixed)
    scratch = [
        pltpu.VMEM((2 * rows, tok_rows), F32),
        pltpu.VMEM((tiles * rows, 2 * LANES), BF16),
        pltpu.VMEM((tiles * rows, 2 * LANES), BF16),
    ]
    input_spec, taps_spec = call(
        early_kernel,
        (shape((tiles * rows, 2 * LANES), F32), shape((tiles * taps_rows, 2 * LANES), F32)),
        scratch,
    )(early, first, turn, small, forward)
    result = call(
        late_kernel,
        shape((peers, narrow, 2 * tok_rows), BF16),
        scratch
        + [
            pltpu.VMEM((tiles * rows, 2 * LANES), F32),
            pltpu.VMEM((tiles * rows, 2 * LANES), F32),
            pltpu.VMEM((2 * rows, tok_rows), BF16),
            pltpu.VMEM((2 * rows, tok_rows), BF16),
        ],
    )(late, input_spec, taps_spec, first, last, turn, small, forward, inverse)
    back = exchange(result)
    grad_input, grad_filter = call(
        final_kernel, (shape((tok_rows, chan_width), BF16), shape((tok_rows, chan_width), F32))
    )(back)
    return grad_input.reshape(1, tok_rows, chan_width), grad_filter


def solution(mesh):
    return jax.shard_map(
        per_device,
        mesh=mesh,
        in_specs=(
            P("rep", "seq", "chan"),
            P("rep", "seq", "chan"),
            P("seq", "chan"),
            P("chan", None),
        ),
        out_specs=(P("rep", "seq", "chan"), P("seq", "chan")),
        check_vma=False,
    )
```

```python
import math

import jax
import jax.numpy as jnp
import numpy as np
from jax import lax
from jax.experimental import pallas as pl
from jax.experimental.pallas import tpu as pltpu
from jax.sharding import PartitionSpec as P


LANES = 128
F32 = jnp.float32
BF16 = jnp.bfloat16
VMEM_LIMIT = 48 * 1024 * 1024
CORES = 2
MAX_DIRECT = 4


def split(values):
    high = values.astype(BF16)
    low = (values - high.astype(F32)).astype(BF16)
    return high, low


def split_table(table):
    table = np.asarray(table, np.float32)
    high = table.astype(BF16)
    low = (table - high.astype(np.float32)).astype(BF16)
    return np.stack([high, low])


def phase(numerator, modulus):
    angle = 2.0 * math.pi * np.mod(numerator, modulus) / modulus
    return np.cos(angle), np.sin(angle)


def tables(devices, groups, narrow, tok_rows):
    length = devices * tok_rows
    tiles = tok_rows // LANES
    rows = groups * devices * narrow
    dev = np.arange(devices)
    quarter = 4 * dev + 1
    cos_d, sin_d = phase(quarter[:, None] * dev[None, :], 4 * devices)
    eye_g, eye_c = np.eye(groups), np.eye(narrow)

    def expand(square):
        return np.einsum("gh,jd,ce->gjchde", eye_g, square, eye_c).reshape(rows, rows)

    cos_d, sin_d = expand(cos_d), expand(sin_d)
    first = split_table(np.concatenate([cos_d, -sin_d], axis=0))
    last = split_table(np.concatenate([cos_d.T, -sin_d.T], axis=1) / length)
    local = np.arange(tok_rows)
    cos_r, sin_r = phase(quarter[:, None] * local[None, :], 4 * length)

    def widen(block):
        block = np.broadcast_to(block[None, :, None, :], (groups, devices, narrow, tok_rows))
        return block.reshape(rows, tok_rows)

    turn = np.stack([widen(cos_r), widen(sin_r)]).astype(np.float32)
    lane = np.arange(LANES)
    step = np.arange(tiles)
    cos_s, sin_s = phase(step[:, None] * lane[None, :], tok_rows)
    small = np.stack([cos_s, sin_s]).astype(np.float32)
    cos_b, sin_b = phase(lane[:, None] * lane[None, :], LANES)
    forward = split_table(np.block([[cos_b, -sin_b], [sin_b, cos_b]]))
    inverse = split_table(np.block([[cos_b, sin_b], [-sin_b, cos_b]]))
    return first, last, turn, small, forward, inverse


def butterflies(real_parts, imag_parts, sign):
    size = len(real_parts)
    if size == 1:
        return real_parts, imag_parts
    even_re, even_im = butterflies(real_parts[0::2], imag_parts[0::2], sign)
    odd_re, odd_im = butterflies(real_parts[1::2], imag_parts[1::2], sign)
    low_re, low_im, high_re, high_im = [], [], [], []
    for index in range(size // 2):
        re, im = odd_re[index], odd_im[index]
        if index == 0:
            turned = (re, im)
        elif 4 * index == size:
            turned = (-im, re) if sign > 0 else (im, -re)
        else:
            angle = sign * 2.0 * math.pi * index / size
            c, s = math.cos(angle), math.sin(angle)
            if 8 * index == size:
                turned = ((re - im) * c, (re + im) * c) if sign > 0 else ((re + im) * c, (im - re) * c)
            else:
                turned = (re * c - im * s, re * s + im * c)
        low_re.append(even_re[index] + turned[0])
        low_im.append(even_im[index] + turned[1])
        high_re.append(even_re[index] - turned[0])
        high_im.append(even_im[index] - turned[1])
    return low_re + high_re, low_im + high_im


def dot(lhs, rhs):
    return jnp.dot(lhs, rhs, preferred_element_type=F32)


CHUNK = 16


def transform(block, first, turn, small, forward, stage, high, low, spectrum, rows, all_rows):
    tiles = block.shape[1] // LANES
    if rows == all_rows:
        stage[...] = dot(first[0], block) + dot(first[1], block)
    else:
        for part in range(2):
            pick = pl.ds(part * all_rows, rows)
            stage[part * rows : (part + 1) * rows, :] = dot(first[0, pick, :rows], block) + dot(
                first[1, pick, :rows], block
            )

    def body(index, carry):
        start = pl.multiple_of(index * CHUNK, CHUNK)
        res, ims = [], []
        for tile in range(tiles):
            lanes = pl.ds(tile * LANES, LANES)
            re = stage[pl.ds(start, CHUNK), lanes]
            im = stage[pl.ds(rows + start, CHUNK), lanes]
            c = turn[0, pl.ds(start, CHUNK), lanes]
            s = turn[1, pl.ds(start, CHUNK), lanes]
            res.append(re * c + im * s)
            ims.append(im * c - re * s)
        res, ims = butterflies(res, ims, -1.0)
        for tile in range(tiles):
            re, im = res[tile], ims[tile]
            if tile > 0:
                c, s = small[0, tile : tile + 1, :], small[1, tile : tile + 1, :]
                re, im = re * c + im * s, im * c - re * s
            at = pl.ds(tile * rows + start, CHUNK)
            for part, lanes in ((re, pl.ds(0, LANES)), (im, pl.ds(LANES, LANES))):
                part_high, part_low = split(part)
                high[at, lanes] = part_high
                low[at, lanes] = part_low
        return carry

    lax.fori_loop(0, rows // CHUNK, body, 0)
    count = tiles * rows
    wide = high[:count, :]
    spectrum[...] = dot(wide, forward[0]) + (dot(wide, forward[1]) + dot(low[:count, :], forward[0]))


def untransform(last, turn, small, inverse, stage, high, low, back_high, back_low, rows, all_rows, tiles):
    count = tiles * rows
    wide = high[:count, :]
    stage[:count, :] = dot(wide, inverse[0]) + (dot(wide, inverse[1]) + dot(low[:count, :], inverse[0]))

    def body(index, carry):
        start = pl.multiple_of(index * CHUNK, CHUNK)
        res, ims = [], []
        for tile in range(tiles):
            at = pl.ds(tile * rows + start, CHUNK)
            re = stage[at, pl.ds(0, LANES)]
            im = stage[at, pl.ds(LANES, LANES)]
            if tile > 0:
                c, s = small[0, tile : tile + 1, :], small[1, tile : tile + 1, :]
                re, im = re * c - im * s, im * c + re * s
            res.append(re)
            ims.append(im)
        res, ims = butterflies(res, ims, 1.0)
        for tile in range(tiles):
            lanes = pl.ds(tile * LANES, LANES)
            c = turn[0, pl.ds(start, CHUNK), lanes]
            s = turn[1, pl.ds(start, CHUNK), lanes]
            re, im = res[tile], ims[tile]
            for part, at in ((re * c - im * s, start), (im * c + re * s, rows + start)):
                part_high, part_low = split(part)
                back_high[pl.ds(at, CHUNK), lanes] = part_high
                back_low[pl.ds(at, CHUNK), lanes] = part_low
        return carry

    lax.fori_loop(0, rows // CHUNK, body, 0)
    if rows == all_rows:
        table_high, table_low = last[0], last[1]
    else:
        table_high, table_low = (
            jnp.concatenate([last[k, :rows, :rows], last[k, :rows, all_rows : all_rows + rows]], axis=1)
            for k in range(2)
        )
    right = back_high[: 2 * rows, :]
    return dot(table_high, right) + (dot(table_low, right) + dot(table_high, back_low[: 2 * rows, :]))


def identity(size, dtype):
    row = lax.broadcasted_iota(jnp.int32, (size, size), 0)
    col = lax.broadcasted_iota(jnp.int32, (size, size), 1)
    return (row == col).astype(dtype)


def flipped(left, right):
    return lax.dot_general(left, right, (((1,), (1,)), ((), ())), preferred_element_type=F32)


def per_device_wide(inputs, cotangent, filter_taps, out_proj):
    devices = lax.axis_size("seq")
    groups = lax.axis_size("rep")
    chans = lax.axis_size("chan")
    tok_rows, chan_width = inputs.shape[1:]
    tiles = tok_rows // LANES
    narrow = chan_width // devices
    rows = chan_width
    first, last, turn, small, forward, inverse = (
        jnp.asarray(t) for t in tables(devices, 1, narrow, tok_rows)
    )
    shape = jax.ShapeDtypeStruct

    def call(kernel, out_shape, scratch=(), cost=3 * 10**6):
        return pl.pallas_call(
            kernel,
            out_shape=out_shape,
            scratch_shapes=scratch,
            compiler_params=pltpu.CompilerParams(vmem_limit_bytes=VMEM_LIMIT),
            cost_estimate=pl.CostEstimate(flops=10**8, bytes_accessed=cost, transcendentals=0),
        )

    def pieces(width):
        return (shape((devices, narrow, width), BF16),)

    def put(out_refs, source, lanes):
        out_refs[0][:, :, lanes] = source[...].reshape(devices, narrow, tok_rows).astype(BF16)

    def take(in_refs, lanes, block):
        block[...] = in_refs[0][:, :, lanes].astype(F32).reshape(rows, tok_rows).astype(BF16)

    def exchange(sent):
        return (lax.all_to_all(sent[0], "seq", split_axis=0, concat_axis=0, tiled=True),)

    count = 1
    front, behind = pl.ds(0, tok_rows), pl.ds(tok_rows, tok_rows)
    flat = pltpu.VMEM((rows, tok_rows), F32)
    block_scratch = pltpu.VMEM((rows, tok_rows), BF16)
    half_pair = [
        pltpu.VMEM((tiles * rows, 2 * LANES), BF16),
        pltpu.VMEM((tiles * rows, 2 * LANES), BF16),
    ]
    back_pair = [
        pltpu.VMEM((2 * rows, tok_rows), BF16),
        pltpu.VMEM((2 * rows, tok_rows), BF16),
    ]
    stage_scratch = pltpu.VMEM((2 * rows, tok_rows), F32)
    spec_shape = shape((tiles * rows, 2 * LANES), F32)
    spec_scratch = pltpu.VMEM((tiles * rows, 2 * LANES), F32)

    def pack_kernel(input_ref, taps_ref, *refs):
        *out_refs, wide = refs
        eye = identity(chan_width, BF16)
        wide[...] = flipped(eye, input_ref[...])
        put(out_refs, wide, front)
        wide[...] = flipped(eye, taps_ref[...])
        put(out_refs, wide, behind)

    def mix_kernel(own_ref, other_ref, proj_ref, *refs):
        *out_refs, wide = refs
        chan = lax.axis_index("chan")
        own = pl.ds(pl.multiple_of(chan * chan_width, chan_width), chan_width)
        other = pl.ds(pl.multiple_of((1 - chan) * chan_width, chan_width), chan_width)
        wide[...] = flipped(proj_ref[:, own], own_ref[...]) + flipped(proj_ref[:, other], other_ref[...])
        put(out_refs, wide, front)

    def early_kernel(*refs):
        recv, (first, turn, small, forward, input_ref, taps_ref, block, stage, high, low) = (
            refs[:count], refs[count:],
        )
        for lanes, spectrum in ((front, input_ref), (behind, taps_ref)):
            take(recv, lanes, block)
            transform(block[...], first, turn, small, forward, stage, high, low, spectrum, rows, rows)

    real, imag = pl.ds(0, LANES), pl.ds(LANES, LANES)

    def multiply(grad, other, high, low):
        def body(tile, carry):
            at = pl.ds(pl.multiple_of(tile * rows, rows), rows)
            gr, gi = grad[at, real], grad[at, imag]
            kr, ki = other[at, real], other[at, imag]
            for part, lanes in ((gr * kr + gi * ki, real), (gi * kr - gr * ki, imag)):
                part_high, part_low = split(part)
                high[at, lanes] = part_high
                low[at, lanes] = part_low
            return carry

        lax.fori_loop(0, tiles, body, 0)

    def filter_kernel(*refs):
        recv, rest = refs[:count], refs[count:]
        (input_ref, first, last, turn, small, forward, inverse, grad, out_ref,
         block, stage, high, low, back, back_high, back_low) = rest
        take(recv, front, block)
        transform(block[...], first, turn, small, forward, stage, high, low, grad, rows, rows)
        multiply(grad, input_ref, high, low)
        value = untransform(
            last, turn, small, inverse, back, high, low, back_high, back_low, rows, rows, tiles
        )
        out_ref[...] = value.astype(BF16)

    def input_kernel(grad, taps_ref, last, turn, small, inverse, *refs):
        *out_refs, high, low, back, back_high, back_low, wide = refs
        multiply(grad, taps_ref, high, low)
        wide[...] = untransform(
            last, turn, small, inverse, back, high, low, back_high, back_low, rows, rows, tiles
        )
        put(out_refs, wide, front)

    def sum_kernel(own_ref, other_ref, *refs):
        *out_refs, wide = refs
        wide[...] = own_ref[...].astype(F32) + other_ref[...].astype(F32)
        put(out_refs, wide, front)

    def final_kernel(*refs):
        *recv, out_ref, block = refs
        take(recv, front, block)
        moved = lax.dot_general(
            block[...], identity(chan_width, BF16), (((0,), (0,)), ((), ())), preferred_element_type=F32
        )
        out_ref[...] = moved.astype(out_ref.dtype)

    own = cotangent.reshape(tok_rows, chan_width)
    other = lax.ppermute(own, "chan", [(k, (k + 1) % chans) for k in range(chans)])
    early = exchange(
        call(pack_kernel, pieces(2 * tok_rows), [flat])(inputs.reshape(tok_rows, chan_width), filter_taps)
    )
    late = exchange(call(mix_kernel, pieces(tok_rows), [flat])(own, other, out_proj))
    input_spec, taps_spec = call(
        early_kernel, (spec_shape, spec_shape), [block_scratch, stage_scratch] + half_pair, 9 * 10**6
    )(*early, first, turn, small, forward)
    grad_spec, partial = call(
        filter_kernel,
        (spec_shape, shape((rows, tok_rows), BF16)),
        [block_scratch, stage_scratch] + half_pair + [spec_scratch] + back_pair,
        9 * 10**6,
    )(*late, input_spec, first, last, turn, small, forward, inverse)
    partial_other = lax.ppermute(partial, "rep", [(k, (k + 1) % groups) for k in range(groups)])
    input_back = exchange(
        call(input_kernel, pieces(tok_rows), half_pair + [spec_scratch] + back_pair + [flat], 6 * 10**6)(
            grad_spec, taps_spec, last, turn, small, inverse
        )
    )
    filter_back = exchange(call(sum_kernel, pieces(tok_rows), [flat])(partial, partial_other))
    grad_input = call(final_kernel, shape((tok_rows, chan_width), BF16), [block_scratch])(*input_back)
    grad_filter = call(final_kernel, shape((tok_rows, chan_width), F32), [block_scratch])(*filter_back)
    return grad_input.reshape(1, tok_rows, chan_width), grad_filter


def per_device_near(inputs, cotangent, filter_taps, out_proj):
    devices = lax.axis_size("seq")
    tok_rows, chan_width = inputs.shape[1:]
    tiles = tok_rows // LANES
    narrow = chan_width // devices
    rows = chan_width
    chips = devices // CORES
    wide_rows = CORES * narrow
    half = chips * narrow
    first, last, turn, small, forward, inverse = (
        jnp.asarray(t) for t in tables(devices, 1, narrow, tok_rows)
    )
    shape = jax.ShapeDtypeStruct
    swap_pairs = [(k, k ^ 1) for k in range(devices)]

    def call(kernel, out_shape, scratch=(), cost=3 * 10**6):
        return pl.pallas_call(
            kernel,
            out_shape=out_shape,
            scratch_shapes=scratch,
            compiler_params=pltpu.CompilerParams(vmem_limit_bytes=VMEM_LIMIT),
            cost_estimate=pl.CostEstimate(flops=10**8, bytes_accessed=cost, transcendentals=0),
        )

    def swap(value):
        return lax.ppermute(value, "seq", swap_pairs)

    def cross(value, axis):
        size = lax.axis_size(axis)
        return lax.ppermute(value, axis, [(k, (k + 1) % size) for k in range(size)])

    def exchange(sent):
        got = [sent[0]]
        for offset in range(1, chips):
            pairs = [(k, k ^ (offset * CORES)) for k in range(devices)]
            got.append(lax.ppermute(sent[offset], "seq", pairs))
        return tuple(got)

    def place():
        at = lax.axis_index("seq")
        return at // CORES, at % CORES

    def pieces(width):
        return tuple(shape((CORES, narrow, width), BF16) for _ in range(chips))

    front, behind = pl.ds(0, tok_rows), pl.ds(tok_rows, tok_rows)
    block_scratch = pltpu.VMEM((rows, tok_rows), BF16)
    half_pair = [
        pltpu.VMEM((tiles * rows, 2 * LANES), BF16),
        pltpu.VMEM((tiles * rows, 2 * LANES), BF16),
    ]
    back_pair = [
        pltpu.VMEM((2 * rows, tok_rows), BF16),
        pltpu.VMEM((2 * rows, tok_rows), BF16),
    ]
    stage_scratch = pltpu.VMEM((2 * rows, tok_rows), F32)
    spec_shape = shape((tiles * rows, 2 * LANES), F32)
    spec_scratch = pltpu.VMEM((tiles * rows, 2 * LANES), F32)
    flat = pltpu.VMEM((rows, tok_rows), F32)
    half_scratch = pltpu.VMEM((half, tok_rows), F32)
    halves = (shape((chips, narrow, tok_rows), BF16), shape((chips, narrow, tok_rows), BF16))

    def put(out_refs, source, side, lanes):
        chip, _ = place()
        for offset in range(chips):
            at = pl.multiple_of((chip ^ offset) * narrow, narrow)
            out_refs[offset][pl.ds(side, 1), :, lanes] = (
                source[pl.ds(at, narrow), :].reshape(1, narrow, tok_rows).astype(BF16)
            )

    def take(in_refs, lanes, block):
        chip, _ = place()
        for offset in range(chips):
            at = pl.multiple_of((chip ^ offset) * wide_rows, wide_rows)
            for core in range(CORES):
                block[pl.ds(at + core * narrow, narrow), :] = in_refs[offset][core, :, lanes]

    def cut(source, mine_ref, theirs_ref):
        _, core = place()
        for chip in range(chips):
            for ref, side in ((mine_ref, core), (theirs_ref, 1 - core)):
                at = pl.multiple_of(chip * wide_rows + side * narrow, narrow)
                ref[chip] = source[pl.ds(at, narrow), :].astype(BF16)

    def chosen(core):
        row = lax.broadcasted_iota(jnp.int32, (half, chan_width), 0)
        col = lax.broadcasted_iota(jnp.int32, (half, chan_width), 1)
        pick = (row // narrow) * wide_rows + core * narrow + row % narrow
        return (pick == col).astype(F32).astype(BF16)

    def pack_kernel(input_ref, input_near, taps_ref, taps_near, *refs):
        *out_refs, wide = refs
        _, core = place()
        pick = chosen(core)
        for own_ref, near_ref, lanes in ((input_ref, input_near, front), (taps_ref, taps_near, behind)):
            for ref, side in ((own_ref, core), (near_ref, 1 - core)):
                wide[...] = flipped(pick, ref[...])
                put(out_refs, wide, side, lanes)

    def own_kernel(own_ref, near_ref, proj_ref, part_ref, part_near, other_ref):
        chan = lax.axis_index("chan")
        _, core = place()
        picked = [
            proj_ref[pl.ds(pl.multiple_of(chip * wide_rows + core * narrow, narrow), narrow), :]
            for chip in range(chips)
        ]
        held = jnp.concatenate(picked, axis=0)
        swapped = jnp.concatenate([held[:, chan_width:], held[:, :chan_width]], axis=1)
        held = jnp.where(chan == 0, held, swapped)
        part_ref[...] = flipped(held[:, :chan_width], own_ref[...])
        part_near[...] = flipped(held[:, :chan_width], near_ref[...])
        other_ref[...] = held[:, chan_width:]

    def mix_kernel(part_ref, part_near, proj_ref, other_ref, other_near, *refs):
        *out_refs, wide = refs
        _, core = place()
        for part, ref, side in ((part_ref, other_ref, core), (part_near, other_near, 1 - core)):
            wide[...] = part[...] + flipped(proj_ref[...], ref[...])
            put(out_refs, wide, side, front)

    def early_kernel(*refs):
        recv, rest = refs[:chips], refs[chips:]
        first, turn, small, forward, input_ref, taps_ref, block, stage, high, low = rest
        for lanes, spectrum in ((front, input_ref), (behind, taps_ref)):
            take(recv, lanes, block)
            transform(block[...], first, turn, small, forward, stage, high, low, spectrum, rows, rows)

    real, imag = pl.ds(0, LANES), pl.ds(LANES, LANES)

    def multiply(grad, other, high, low):
        def body(tile, carry):
            at = pl.ds(pl.multiple_of(tile * rows, rows), rows)
            gr, gi = grad[at, real], grad[at, imag]
            kr, ki = other[at, real], other[at, imag]
            for part, lanes in ((gr * kr + gi * ki, real), (gi * kr - gr * ki, imag)):
                part_high, part_low = split(part)
                high[at, lanes] = part_high
                low[at, lanes] = part_low
            return carry

        lax.fori_loop(0, tiles, body, 0)

    def filter_kernel(*refs):
        recv, rest = refs[:chips], refs[chips:]
        (input_ref, first, last, turn, small, forward, inverse, grad, mine_ref, theirs_ref,
         block, stage, high, low, back, back_high, back_low, wide) = rest
        take(recv, front, block)
        transform(block[...], first, turn, small, forward, stage, high, low, grad, rows, rows)
        multiply(grad, input_ref, high, low)
        wide[...] = untransform(
            last, turn, small, inverse, back, high, low, back_high, back_low, rows, rows, tiles
        )
        cut(wide, mine_ref, theirs_ref)

    def input_kernel(grad, taps_ref, last, turn, small, inverse, mine_ref, theirs_ref, *scratch):
        high, low, back, back_high, back_low, wide = scratch
        multiply(grad, taps_ref, high, low)
        wide[...] = untransform(
            last, turn, small, inverse, back, high, low, back_high, back_low, rows, rows, tiles
        )
        cut(wide, mine_ref, theirs_ref)

    def join_kernel(mine_ref, near_ref, *out_refs):
        chip, core = place()
        for offset in range(chips):
            for ref, side in ((mine_ref, core), (near_ref, 1 - core)):
                out_refs[offset][pl.ds(side, 1)] = ref[pl.ds(chip ^ offset, 1)]

    def sum_kernel(mine_ref, mine_other, near_ref, near_other, *out_refs):
        chip, core = place()
        for offset in range(chips):
            at = pl.ds(chip ^ offset, 1)
            for ref, other, side in ((mine_ref, mine_other, core), (near_ref, near_other, 1 - core)):
                total = ref[at].astype(F32) + other[at].astype(F32)
                out_refs[offset][pl.ds(side, 1)] = total.astype(BF16)

    def final_kernel(*refs):
        *recv, out_ref, block = refs
        take(recv, front, block)
        moved = lax.dot_general(
            block[...], identity(chan_width, BF16), (((0,), (0,)), ((), ())), preferred_element_type=F32
        )
        out_ref[...] = moved.astype(out_ref.dtype)

    signal = inputs.reshape(tok_rows, chan_width)
    own = cotangent.reshape(tok_rows, chan_width)
    signal_near = swap(signal)
    taps_near = swap(filter_taps)
    other = cross(own, "chan")
    own_near = swap(own)
    early = exchange(
        call(pack_kernel, pieces(2 * tok_rows), [half_scratch])(signal, signal_near, filter_taps, taps_near),
    )
    part_shape = shape((half, tok_rows), F32)
    part, part_near, proj_other = call(
        own_kernel, (part_shape, part_shape, shape((half, chan_width), BF16))
    )(own, own_near, out_proj)
    other_near = swap(other)
    late = exchange(call(mix_kernel, pieces(tok_rows), [half_scratch])(part, part_near, proj_other, other, other_near))
    input_spec, taps_spec = call(
        early_kernel, (spec_shape, spec_shape), [block_scratch, stage_scratch] + half_pair, 9 * 10**6
    )(*early, first, turn, small, forward)
    grad_spec, mine, theirs = call(
        filter_kernel,
        (spec_shape,) + halves,
        [block_scratch, stage_scratch] + half_pair + [spec_scratch] + back_pair + [flat],
        9 * 10**6,
    )(*late, input_spec, first, last, turn, small, forward, inverse)
    mine_other = cross(mine, "rep")
    near = swap(theirs)
    near_other = cross(near, "rep")
    input_mine, input_theirs = call(
        input_kernel, halves, half_pair + [spec_scratch] + back_pair + [flat], 6 * 10**6
    )(grad_spec, taps_spec, last, turn, small, inverse)
    input_near = swap(input_theirs)
    input_back = exchange(call(join_kernel, pieces(tok_rows))(input_mine, input_near))
    filter_back = exchange(call(sum_kernel, pieces(tok_rows))(mine, mine_other, near, near_other))
    grad_input = call(final_kernel, shape((tok_rows, chan_width), BF16), [block_scratch])(*input_back)
    grad_filter = call(final_kernel, shape((tok_rows, chan_width), F32), [block_scratch])(*filter_back)
    return grad_input.reshape(1, tok_rows, chan_width), grad_filter


def solution(mesh):
    few = mesh.shape["seq"] == CORES * MAX_DIRECT
    body = per_device_near if few else per_device_wide

    return jax.shard_map(
        body,
        mesh=mesh,
        in_specs=(
            P("rep", "seq", "chan"),
            P("rep", "seq", "chan"),
            P("seq", "chan"),
            P("chan", None),
        ),
        out_specs=(P("rep", "seq", "chan"), P("seq", "chan")),
        check_vma=False,
    )
```

```python
import math

import jax
import jax.numpy as jnp
import numpy as np
from jax import lax
from jax.experimental import pallas as pl
from jax.experimental.pallas import tpu as pltpu
from jax.sharding import PartitionSpec as P


LANES = 128
F32 = jnp.float32
BF16 = jnp.bfloat16
VMEM_LIMIT = 48 * 1024 * 1024
CORES = 2
MAX_DIRECT = 4


def split(values):
    high = values.astype(BF16)
    low = (values - high.astype(F32)).astype(BF16)
    return high, low


def split_table(table):
    table = np.asarray(table, np.float32)
    high = table.astype(BF16)
    low = (table - high.astype(np.float32)).astype(BF16)
    return np.stack([high, low])


def phase(numerator, modulus):
    angle = 2.0 * math.pi * np.mod(numerator, modulus) / modulus
    return np.cos(angle), np.sin(angle)


def tables(devices, groups, narrow, tok_rows):
    length = devices * tok_rows
    tiles = tok_rows // LANES
    rows = groups * devices * narrow
    dev = np.arange(devices)
    quarter = 4 * dev + 1
    cos_d, sin_d = phase(quarter[:, None] * dev[None, :], 4 * devices)
    eye_g, eye_c = np.eye(groups), np.eye(narrow)

    def expand(square):
        return np.einsum("gh,jd,ce->gjchde", eye_g, square, eye_c).reshape(rows, rows)

    cos_d, sin_d = expand(cos_d), expand(sin_d)
    first = split_table(np.concatenate([cos_d, -sin_d], axis=0))
    last = split_table(np.concatenate([cos_d.T, -sin_d.T], axis=1) / length)
    local = np.arange(tok_rows)
    cos_r, sin_r = phase(quarter[:, None] * local[None, :], 4 * length)

    def widen(block):
        block = np.broadcast_to(block[None, :, None, :], (groups, devices, narrow, tok_rows))
        return block.reshape(rows, tok_rows)

    turn = np.stack([widen(cos_r), widen(sin_r)]).astype(np.float32)
    lane = np.arange(LANES)
    step = np.arange(tiles)
    cos_s, sin_s = phase(step[:, None] * lane[None, :], tok_rows)
    small = np.stack([cos_s, sin_s]).astype(np.float32)
    cos_b, sin_b = phase(lane[:, None] * lane[None, :], LANES)
    forward = split_table(np.block([[cos_b, -sin_b], [sin_b, cos_b]]))
    inverse = split_table(np.block([[cos_b, sin_b], [-sin_b, cos_b]]))
    return first, last, turn, small, forward, inverse


def butterflies(real_parts, imag_parts, sign):
    size = len(real_parts)
    if size == 1:
        return real_parts, imag_parts
    even_re, even_im = butterflies(real_parts[0::2], imag_parts[0::2], sign)
    odd_re, odd_im = butterflies(real_parts[1::2], imag_parts[1::2], sign)
    low_re, low_im, high_re, high_im = [], [], [], []
    for index in range(size // 2):
        re, im = odd_re[index], odd_im[index]
        if index == 0:
            turned = (re, im)
        elif 4 * index == size:
            turned = (-im, re) if sign > 0 else (im, -re)
        else:
            angle = sign * 2.0 * math.pi * index / size
            c, s = math.cos(angle), math.sin(angle)
            if 8 * index == size:
                turned = ((re - im) * c, (re + im) * c) if sign > 0 else ((re + im) * c, (im - re) * c)
            else:
                turned = (re * c - im * s, re * s + im * c)
        low_re.append(even_re[index] + turned[0])
        low_im.append(even_im[index] + turned[1])
        high_re.append(even_re[index] - turned[0])
        high_im.append(even_im[index] - turned[1])
    return low_re + high_re, low_im + high_im


def dot(lhs, rhs):
    return jnp.dot(lhs, rhs, preferred_element_type=F32)


CHUNK = 16


def transform(block, first, turn, small, forward, stage, high, low, spectrum, rows):
    tiles = block.shape[1] // LANES
    table = jnp.concatenate([first[0], first[1]], axis=1)
    stage[...] = dot(table, jnp.concatenate([block, block], axis=0))

    def body(index, carry):
        start = pl.multiple_of(index * CHUNK, CHUNK)
        res, ims = [], []
        for tile in range(tiles):
            lanes = pl.ds(tile * LANES, LANES)
            re = stage[pl.ds(start, CHUNK), lanes]
            im = stage[pl.ds(rows + start, CHUNK), lanes]
            c = turn[0, pl.ds(start, CHUNK), lanes]
            s = turn[1, pl.ds(start, CHUNK), lanes]
            res.append(re * c + im * s)
            ims.append(im * c - re * s)
        res, ims = butterflies(res, ims, -1.0)
        for tile in range(tiles):
            re, im = res[tile], ims[tile]
            if tile > 0:
                c, s = small[0, tile : tile + 1, :], small[1, tile : tile + 1, :]
                re, im = re * c + im * s, im * c - re * s
            at = pl.ds(tile * rows + start, CHUNK)
            for part, lanes in ((re, pl.ds(0, LANES)), (im, pl.ds(LANES, LANES))):
                part_high, part_low = split(part)
                high[at, lanes] = part_high
                low[at, lanes] = part_low
        return carry

    lax.fori_loop(0, rows // CHUNK, body, 0)
    spectrum[...] = dot(
        jnp.concatenate([high[...], low[...], high[...]], axis=1),
        jnp.concatenate([forward[0], forward[0], forward[1]], axis=0),
    )


def untransform(last, turn, small, inverse, stage, high, back_high, rows, tiles):
    stage[...] = dot(
        jnp.concatenate([high[...], high[...]], axis=1),
        jnp.concatenate([inverse[0], inverse[1]], axis=0),
    )

    def body(index, carry):
        start = pl.multiple_of(index * CHUNK, CHUNK)
        res, ims = [], []
        for tile in range(tiles):
            at = pl.ds(tile * rows + start, CHUNK)
            re = stage[at, pl.ds(0, LANES)]
            im = stage[at, pl.ds(LANES, LANES)]
            if tile > 0:
                c, s = small[0, tile : tile + 1, :], small[1, tile : tile + 1, :]
                re, im = re * c - im * s, im * c + re * s
            res.append(re)
            ims.append(im)
        res, ims = butterflies(res, ims, 1.0)
        for tile in range(tiles):
            lanes = pl.ds(tile * LANES, LANES)
            c = turn[0, pl.ds(start, CHUNK), lanes]
            s = turn[1, pl.ds(start, CHUNK), lanes]
            re, im = res[tile], ims[tile]
            back_high[pl.ds(start, CHUNK), lanes] = (re * c - im * s).astype(BF16)
            back_high[pl.ds(rows + start, CHUNK), lanes] = (im * c + re * s).astype(BF16)
        return carry

    lax.fori_loop(0, rows // CHUNK, body, 0)
    right = back_high[...]
    return dot(
        jnp.concatenate([last[0], last[1]], axis=1),
        jnp.concatenate([right, right], axis=0),
    )


def identity(size, dtype):
    row = lax.broadcasted_iota(jnp.int32, (size, size), 0)
    col = lax.broadcasted_iota(jnp.int32, (size, size), 1)
    return (row == col).astype(dtype)


def flipped(left, right):
    return lax.dot_general(left, right, (((1,), (1,)), ((), ())), preferred_element_type=F32)


def per_device_wide(inputs, cotangent, filter_taps, out_proj):
    devices = lax.axis_size("seq")
    groups = lax.axis_size("rep")
    chans = lax.axis_size("chan")
    tok_rows, chan_width = inputs.shape[1:]
    tiles = tok_rows // LANES
    narrow = chan_width // devices
    rows = chan_width
    first, last, turn, small, forward, inverse = (
        jnp.asarray(t) for t in tables(devices, 1, narrow, tok_rows)
    )
    shape = jax.ShapeDtypeStruct

    def call(kernel, out_shape, scratch=(), cost=3 * 10**6):
        return pl.pallas_call(
            kernel,
            out_shape=out_shape,
            scratch_shapes=scratch,
            compiler_params=pltpu.CompilerParams(vmem_limit_bytes=VMEM_LIMIT),
            cost_estimate=pl.CostEstimate(flops=10**8, bytes_accessed=cost, transcendentals=0),
        )

    def pieces(width):
        return (shape((devices, narrow, width), BF16),)

    def put(out_refs, source, lanes):
        out_refs[0][:, :, lanes] = source[...].reshape(devices, narrow, tok_rows).astype(BF16)

    def take(in_refs, lanes, block):
        block[...] = in_refs[0][:, :, lanes].astype(F32).reshape(rows, tok_rows).astype(BF16)

    def exchange(sent):
        return (lax.all_to_all(sent[0], "seq", split_axis=0, concat_axis=0, tiled=True),)

    count = 1
    front, behind = pl.ds(0, tok_rows), pl.ds(tok_rows, tok_rows)
    flat = pltpu.VMEM((rows, tok_rows), F32)
    block_scratch = pltpu.VMEM((rows, tok_rows), BF16)
    half_pair = [
        pltpu.VMEM((tiles * rows, 2 * LANES), BF16),
        pltpu.VMEM((tiles * rows, 2 * LANES), BF16),
    ]
    back_one = [pltpu.VMEM((2 * rows, tok_rows), BF16)]
    stage_scratch = pltpu.VMEM((2 * rows, tok_rows), F32)
    spec_shape = shape((tiles * rows, 2 * LANES), F32)
    spec_scratch = pltpu.VMEM((tiles * rows, 2 * LANES), F32)

    def pack_kernel(input_ref, taps_ref, *refs):
        *out_refs, wide = refs
        eye = identity(chan_width, BF16)
        wide[...] = flipped(eye, input_ref[...])
        put(out_refs, wide, front)
        wide[...] = flipped(eye, taps_ref[...])
        put(out_refs, wide, behind)

    def mix_kernel(own_ref, other_ref, proj_ref, *refs):
        *out_refs, wide = refs
        chan = lax.axis_index("chan")
        own = pl.ds(pl.multiple_of(chan * chan_width, chan_width), chan_width)
        other = pl.ds(pl.multiple_of((1 - chan) * chan_width, chan_width), chan_width)
        wide[...] = flipped(proj_ref[:, own], own_ref[...]) + flipped(proj_ref[:, other], other_ref[...])
        put(out_refs, wide, front)

    def early_kernel(*refs):
        recv, (first, turn, small, forward, input_ref, taps_ref, block, stage, high, low) = (
            refs[:count], refs[count:],
        )
        for lanes, spectrum in ((front, input_ref), (behind, taps_ref)):
            take(recv, lanes, block)
            transform(block[...], first, turn, small, forward, stage, high, low, spectrum, rows)

    real, imag = pl.ds(0, LANES), pl.ds(LANES, LANES)

    def multiply(grad, other, high):
        def body(tile, carry):
            at = pl.ds(pl.multiple_of(tile * rows, rows), rows)
            gr, gi = grad[at, real], grad[at, imag]
            kr, ki = other[at, real], other[at, imag]
            high[at, real] = (gr * kr + gi * ki).astype(BF16)
            high[at, imag] = (gi * kr - gr * ki).astype(BF16)
            return carry

        lax.fori_loop(0, tiles, body, 0)

    def filter_kernel(*refs):
        recv, rest = refs[:count], refs[count:]
        (input_ref, first, last, turn, small, forward, inverse, grad, out_ref,
         block, stage, high, low, back, back_high) = rest
        take(recv, front, block)
        transform(block[...], first, turn, small, forward, stage, high, low, grad, rows)
        multiply(grad, input_ref, high)
        value = untransform(
            last, turn, small, inverse, back, high, back_high, rows, tiles
        )
        out_ref[...] = value.astype(BF16)

    def input_kernel(grad, taps_ref, last, turn, small, inverse, *refs):
        *out_refs, high, low, back, back_high, wide = refs
        multiply(grad, taps_ref, high)
        wide[...] = untransform(
            last, turn, small, inverse, back, high, back_high, rows, tiles
        )
        put(out_refs, wide, front)

    def sum_kernel(own_ref, other_ref, *refs):
        *out_refs, wide = refs
        wide[...] = own_ref[...].astype(F32) + other_ref[...].astype(F32)
        put(out_refs, wide, front)

    def final_kernel(*refs):
        *recv, out_ref, block = refs
        take(recv, front, block)
        moved = lax.dot_general(
            block[...], identity(chan_width, BF16), (((0,), (0,)), ((), ())), preferred_element_type=F32
        )
        out_ref[...] = moved.astype(out_ref.dtype)

    own = cotangent.reshape(tok_rows, chan_width)
    other = lax.ppermute(own, "chan", [(k, (k + 1) % chans) for k in range(chans)])
    early = exchange(
        call(pack_kernel, pieces(2 * tok_rows), [flat])(inputs.reshape(tok_rows, chan_width), filter_taps)
    )
    late = exchange(call(mix_kernel, pieces(tok_rows), [flat])(own, other, out_proj))
    input_spec, taps_spec = call(
        early_kernel, (spec_shape, spec_shape), [block_scratch, stage_scratch] + half_pair, 9 * 10**6
    )(*early, first, turn, small, forward)
    grad_spec, partial = call(
        filter_kernel,
        (spec_shape, shape((rows, tok_rows), BF16)),
        [block_scratch, stage_scratch] + half_pair + [spec_scratch] + back_one,
        9 * 10**6,
    )(*late, input_spec, first, last, turn, small, forward, inverse)
    partial_other = lax.ppermute(partial, "rep", [(k, (k + 1) % groups) for k in range(groups)])
    input_back = exchange(
        call(input_kernel, pieces(tok_rows), half_pair + [spec_scratch] + back_one + [flat], 6 * 10**6)(
            grad_spec, taps_spec, last, turn, small, inverse
        )
    )
    filter_back = exchange(call(sum_kernel, pieces(tok_rows), [flat])(partial, partial_other))
    grad_input = call(final_kernel, shape((tok_rows, chan_width), BF16), [block_scratch])(*input_back)
    grad_filter = call(final_kernel, shape((tok_rows, chan_width), F32), [block_scratch])(*filter_back)
    return grad_input.reshape(1, tok_rows, chan_width), grad_filter


def per_device_near(inputs, cotangent, filter_taps, out_proj):
    devices = lax.axis_size("seq")
    groups = lax.axis_size("rep")
    tok_rows, chan_width = inputs.shape[1:]
    tiles = tok_rows // LANES
    narrow = chan_width // devices
    rows = chan_width
    chips = devices // CORES
    wide_rows = CORES * narrow
    half = chips * narrow
    first, last, turn, small, forward, inverse = (
        jnp.asarray(t) for t in tables(devices, 1, narrow, tok_rows)
    )
    shape = jax.ShapeDtypeStruct
    swap_pairs = [(k, k ^ 1) for k in range(devices)]

    def call(kernel, out_shape, scratch=(), cost=3 * 10**6):
        return pl.pallas_call(
            kernel,
            out_shape=out_shape,
            scratch_shapes=scratch,
            compiler_params=pltpu.CompilerParams(vmem_limit_bytes=VMEM_LIMIT),
            cost_estimate=pl.CostEstimate(flops=10**8, bytes_accessed=cost, transcendentals=0),
        )

    def swap(value):
        return lax.ppermute(value, "seq", swap_pairs)

    def cross(value, axis):
        size = lax.axis_size(axis)
        return lax.ppermute(value, axis, [(k, (k + 1) % size) for k in range(size)])

    def exchange(sent):
        got = [sent[0]]
        for offset in range(1, chips):
            pairs = [(k, k ^ (offset * CORES)) for k in range(devices)]
            got.append(lax.ppermute(sent[offset], "seq", pairs))
        return tuple(got)

    def place():
        at = lax.axis_index("seq")
        return at // CORES, at % CORES

    def pieces(width):
        return tuple(shape((CORES, narrow, width), BF16) for _ in range(chips))

    part_rows = tok_rows // groups
    front, behind = pl.ds(0, tok_rows), pl.ds(tok_rows, part_rows)
    block_scratch = pltpu.VMEM((rows, tok_rows), BF16)
    half_pair = [
        pltpu.VMEM((tiles * rows, 2 * LANES), BF16),
        pltpu.VMEM((tiles * rows, 2 * LANES), BF16),
    ]
    back_one = [pltpu.VMEM((2 * rows, tok_rows), BF16)]
    stage_scratch = pltpu.VMEM((2 * rows, tok_rows), F32)
    spec_shape = shape((tiles * rows, 2 * LANES), F32)
    spec_scratch = pltpu.VMEM((tiles * rows, 2 * LANES), F32)
    flat = pltpu.VMEM((rows, tok_rows), F32)
    half_scratch = pltpu.VMEM((half, tok_rows), F32)
    halves = (shape((chips, narrow, tok_rows), BF16), shape((chips, narrow, tok_rows), BF16))

    def put(out_refs, source, side, lanes, part=slice(None)):
        chip, _ = place()
        for offset in range(chips):
            at = pl.multiple_of((chip ^ offset) * narrow, narrow)
            out_refs[offset][pl.ds(side, 1), :, lanes] = (
                source[pl.ds(at, narrow), part][None].astype(BF16)
            )

    def take(in_refs, lanes, block):
        chip, _ = place()
        for offset in range(chips):
            at = pl.multiple_of((chip ^ offset) * wide_rows, wide_rows)
            for core in range(CORES):
                block[pl.ds(at + core * narrow, narrow), :] = in_refs[offset][core, :, lanes]

    def cut(source, mine_ref, theirs_ref):
        _, core = place()
        for chip in range(chips):
            for ref, side in ((mine_ref, core), (theirs_ref, 1 - core)):
                at = pl.multiple_of(chip * wide_rows + side * narrow, narrow)
                ref[chip] = source[pl.ds(at, narrow), :].astype(BF16)

    def chosen(core):
        row = lax.broadcasted_iota(jnp.int32, (half, chan_width), 0)
        col = lax.broadcasted_iota(jnp.int32, (half, chan_width), 1)
        pick = (row // narrow) * wide_rows + core * narrow + row % narrow
        return (pick == col).astype(F32).astype(BF16)

    def pack_kernel(held_ref, input_near, taps_near, *refs):
        *out_refs, wide = refs
        _, core = place()
        pick = chosen(core)
        start = pl.multiple_of(lax.axis_index("rep") * part_rows, part_rows)
        wide[...] = flipped(pick, held_ref[:tok_rows, :])
        put(out_refs, wide, core, front)
        wide[...] = flipped(pick, input_near[...])
        put(out_refs, wide, 1 - core, front)
        part = pl.ds(0, part_rows)
        wide[:, part] = flipped(pick, held_ref[tok_rows:, :])
        put(out_refs, wide, core, behind, part)
        wide[:, part] = flipped(pick, taps_near[pl.ds(start, part_rows), :])
        put(out_refs, wide, 1 - core, behind, part)

    def taps_kernel(gate_ref, *refs):
        *recv, out_ref = refs
        take(recv, behind, out_ref)

    def own_kernel(own_ref, proj_ref, near_ref, part_ref, part_near, other_ref):
        chan = lax.axis_index("chan")
        _, core = place()
        picked = [
            proj_ref[pl.ds(pl.multiple_of(chip * wide_rows + core * narrow, narrow), narrow), :]
            for chip in range(chips)
        ]
        held = jnp.concatenate(picked, axis=0)
        swapped = jnp.concatenate([held[:, chan_width:], held[:, :chan_width]], axis=1)
        held = jnp.where(chan == 0, held, swapped)
        part_ref[...] = flipped(held[:, :chan_width], own_ref[...])
        part_near[...] = flipped(held[:, :chan_width], near_ref[...])
        other_ref[...] = held[:, chan_width:]

    def mix_kernel(part_ref, part_near, proj_ref, other_ref, other_near, *refs):
        *out_refs, wide = refs
        _, core = place()
        for part, ref, side in ((part_ref, other_ref, core), (part_near, other_near, 1 - core)):
            wide[...] = part[...] + flipped(proj_ref[...], ref[...])
            put(out_refs, wide, side, front)

    def signal_kernel(*refs):
        recv, (first, turn, small, forward, spectrum, block, stage, high, low) = refs[:chips], refs[chips:]
        take(recv, front, block)
        transform(block[...], first, turn, small, forward, stage, high, low, spectrum, rows)

    def taps_spec_kernel(own_ref, other_ref, first, turn, small, forward, spectrum, block, stage, high, low):
        index = lax.axis_index("rep")
        for ref, at in ((own_ref, index), (other_ref, 1 - index)):
            block[:, pl.ds(pl.multiple_of(at * part_rows, part_rows), part_rows)] = ref[...]
        transform(block[...], first, turn, small, forward, stage, high, low, spectrum, rows)

    real, imag = pl.ds(0, LANES), pl.ds(LANES, LANES)

    def multiply(grad, other, high):
        def body(tile, carry):
            at = pl.ds(pl.multiple_of(tile * rows, rows), rows)
            gr, gi = grad[at, real], grad[at, imag]
            kr, ki = other[at, real], other[at, imag]
            high[at, real] = (gr * kr + gi * ki).astype(BF16)
            high[at, imag] = (gi * kr - gr * ki).astype(BF16)
            return carry

        lax.fori_loop(0, tiles, body, 0)

    def filter_kernel(*refs):
        recv, rest = refs[:chips], refs[chips:]
        (input_ref, first, last, turn, small, forward, inverse, grad, mine_ref, theirs_ref,
         block, stage, high, low, back, back_high, wide) = rest
        take(recv, front, block)
        transform(block[...], first, turn, small, forward, stage, high, low, grad, rows)
        multiply(grad, input_ref, high)
        wide[...] = untransform(last, turn, small, inverse, back, high, back_high, rows, tiles)
        cut(wide, mine_ref, theirs_ref)

    def input_kernel(grad, taps_ref, last, turn, small, inverse, *refs):
        *out_refs, high, back, back_high, wide = refs
        multiply(grad, taps_ref, high)
        wide[...] = untransform(last, turn, small, inverse, back, high, back_high, rows, tiles)
        chip, _ = place()
        for offset in range(chips):
            at = pl.multiple_of((chip ^ offset) * wide_rows, wide_rows)
            out_refs[offset][...] = (
                wide[pl.ds(at, wide_rows), :].reshape(CORES, narrow, tok_rows).astype(BF16)
            )

    def gate_kernel(value_ref, out_ref):
        out_ref[...] = value_ref[:16, :]

    def sum_kernel(mine_ref, mine_other, near_ref, near_other, *out_refs):
        chip, core = place()
        for offset in range(chips):
            at = pl.ds(chip ^ offset, 1)
            for ref, other, side in ((mine_ref, mine_other, core), (near_ref, near_other, 1 - core)):
                total = ref[at].astype(F32) + other[at].astype(F32)
                out_refs[offset][pl.ds(side, 1)] = total.astype(BF16)

    def final_kernel(*refs):
        *recv, out_ref, block = refs
        if len(recv) == chips:
            take(recv, front, block)
        else:
            chip, core = place()
            for offset in range(chips):
                for flip in range(CORES):
                    at = pl.multiple_of((chip ^ offset) * wide_rows + (core ^ flip) * narrow, narrow)
                    block[pl.ds(at, narrow), :] = recv[flip * chips + offset][core]
        moved = lax.dot_general(
            block[...], identity(chan_width, BF16), (((0,), (0,)), ((), ())), preferred_element_type=F32
        )
        out_ref[...] = moved.astype(out_ref.dtype)

    signal = inputs.reshape(tok_rows, chan_width)
    own = cotangent.reshape(tok_rows, chan_width)
    signal_near = swap(signal)
    taps_near = swap(filter_taps)
    other = cross(own, "chan")
    own_near = swap(own)
    taps_part = lax.dynamic_slice_in_dim(filter_taps, lax.axis_index("rep") * part_rows, part_rows, 0)
    held = jnp.concatenate([signal, taps_part], axis=0)
    early = exchange(
        call(
            pack_kernel,
            pieces(tok_rows + part_rows),
            [half_scratch],
        )(held, signal_near, taps_near),
    )
    part_shape = shape((half, tok_rows), F32)
    part, part_near, proj_other = call(
        own_kernel,
        (part_shape, part_shape, shape((half, chan_width), BF16)),
    )(own, out_proj, own_near)
    other_near = swap(other)
    late = exchange(call(mix_kernel, pieces(tok_rows), [half_scratch])(part, part_near, proj_other, other, other_near))
    gate = call(gate_kernel, shape((16, chan_width), BF16), (), 10**4)(proj_other)
    own_taps = call(taps_kernel, shape((rows, part_rows), BF16))(gate, *early)
    other_taps = cross(own_taps, "rep")
    transform_scratch = [block_scratch, stage_scratch] + half_pair
    input_spec = call(signal_kernel, spec_shape, transform_scratch, 6 * 10**6)(
        *early, first, turn, small, forward
    )
    grad_spec, mine, theirs = call(
        filter_kernel,
        (spec_shape,) + halves,
        [block_scratch, stage_scratch] + half_pair + [spec_scratch] + back_one + [flat],
        12 * 10**6,
    )(*late, input_spec, first, last, turn, small, forward, inverse)
    mine_other = cross(mine, "rep")
    near = swap(theirs)
    near_other = cross(near, "rep")
    taps_spec = call(taps_spec_kernel, spec_shape, transform_scratch, 6 * 10**6)(
        own_taps, other_taps, first, turn, small, forward
    )
    input_sent = call(
        input_kernel, pieces(tok_rows), half_pair[:1] + [spec_scratch] + back_one + [flat], 6 * 10**6
    )(grad_spec, taps_spec, last, turn, small, inverse)
    input_back = exchange(input_sent)
    input_back += tuple(swap(piece) for piece in input_back)
    filter_back = exchange(call(sum_kernel, pieces(tok_rows))(mine, mine_other, near, near_other))
    grad_input = call(final_kernel, shape((tok_rows, chan_width), BF16), [block_scratch])(*input_back)
    grad_filter = call(final_kernel, shape((tok_rows, chan_width), F32), [block_scratch])(*filter_back)
    return grad_input.reshape(1, tok_rows, chan_width), grad_filter


def solution(mesh):
    few = mesh.shape["seq"] == CORES * MAX_DIRECT
    body = per_device_near if few else per_device_wide

    return jax.shard_map(
        body,
        mesh=mesh,
        in_specs=(
            P("rep", "seq", "chan"),
            P("rep", "seq", "chan"),
            P("seq", "chan"),
            P("chan", None),
        ),
        out_specs=(P("rep", "seq", "chan"), P("seq", "chan")),
        check_vma=False,
    )
```

```python
import math

import jax
import jax.numpy as jnp
import numpy as np
from jax import lax
from jax.experimental import pallas as pl
from jax.experimental.pallas import tpu as pltpu
from jax.sharding import PartitionSpec as P


LANES = 128
F32 = jnp.float32
BF16 = jnp.bfloat16
VMEM_LIMIT = 48 * 1024 * 1024
CORES = 2
MAX_DIRECT = 4


def split(values):
    high = values.astype(BF16)
    low = (values - high.astype(F32)).astype(BF16)
    return high, low


def split_table(table):
    table = np.asarray(table, np.float32)
    high = table.astype(BF16)
    low = (table - high.astype(np.float32)).astype(BF16)
    return np.stack([high, low])


def phase(numerator, modulus):
    angle = 2.0 * math.pi * np.mod(numerator, modulus) / modulus
    return np.cos(angle), np.sin(angle)


def tables(devices, groups, narrow, tok_rows):
    length = devices * tok_rows
    tiles = tok_rows // LANES
    rows = groups * devices * narrow
    dev = np.arange(devices)
    quarter = 4 * dev + 1
    cos_d, sin_d = phase(quarter[:, None] * dev[None, :], 4 * devices)
    eye_g, eye_c = np.eye(groups), np.eye(narrow)

    def expand(square):
        return np.einsum("gh,jd,ce->gjchde", eye_g, square, eye_c).reshape(rows, rows)

    cos_d, sin_d = expand(cos_d), expand(sin_d)
    first = split_table(np.concatenate([cos_d, -sin_d], axis=0))
    last = split_table(np.concatenate([cos_d.T, -sin_d.T], axis=1) / length)
    local = np.arange(tok_rows)
    cos_r, sin_r = phase(quarter[:, None] * local[None, :], 4 * length)

    def widen(block):
        block = np.broadcast_to(block[None, :, None, :], (groups, devices, narrow, tok_rows))
        return block.reshape(rows, tok_rows)

    turn = np.stack([widen(cos_r), widen(sin_r)]).astype(np.float32)
    lane = np.arange(LANES)
    step = np.arange(tiles)
    cos_s, sin_s = phase(step[:, None] * lane[None, :], tok_rows)
    small = np.stack([cos_s, sin_s]).astype(np.float32)
    cos_b, sin_b = phase(lane[:, None] * lane[None, :], LANES)
    forward = split_table(np.block([[cos_b, -sin_b], [sin_b, cos_b]]))
    inverse = split_table(np.block([[cos_b, sin_b], [-sin_b, cos_b]]))
    return first, last, turn, small, forward, inverse


def butterflies(real_parts, imag_parts, sign):
    size = len(real_parts)
    if size == 1:
        return real_parts, imag_parts
    even_re, even_im = butterflies(real_parts[0::2], imag_parts[0::2], sign)
    odd_re, odd_im = butterflies(real_parts[1::2], imag_parts[1::2], sign)
    low_re, low_im, high_re, high_im = [], [], [], []
    for index in range(size // 2):
        re, im = odd_re[index], odd_im[index]
        if index == 0:
            turned = (re, im)
        elif 4 * index == size:
            turned = (-im, re) if sign > 0 else (im, -re)
        else:
            angle = sign * 2.0 * math.pi * index / size
            c, s = math.cos(angle), math.sin(angle)
            if 8 * index == size:
                turned = ((re - im) * c, (re + im) * c) if sign > 0 else ((re + im) * c, (im - re) * c)
            else:
                turned = (re * c - im * s, re * s + im * c)
        low_re.append(even_re[index] + turned[0])
        low_im.append(even_im[index] + turned[1])
        high_re.append(even_re[index] - turned[0])
        high_im.append(even_im[index] - turned[1])
    return low_re + high_re, low_im + high_im


def dot(lhs, rhs):
    return jnp.dot(lhs, rhs, preferred_element_type=F32)


CHUNK = 16
GROUP = 32


def spread(block, first, stage):
    table = jnp.concatenate([first[0], first[1]], axis=1)
    stage[...] = dot(table, jnp.concatenate([block, block], axis=0))


def forward_group(group, turn, small, forward, stage, high, low, rows, tiles):
    for start in range(group * GROUP, (group + 1) * GROUP, CHUNK):
        own = slice(start, start + CHUNK)
        res, ims = [], []
        for tile in range(tiles):
            lanes = slice(tile * LANES, (tile + 1) * LANES)
            re = stage[own, lanes]
            im = stage[rows + start : rows + start + CHUNK, lanes]
            c, s = turn[0, own, lanes], turn[1, own, lanes]
            res.append(re * c + im * s)
            ims.append(im * c - re * s)
        res, ims = butterflies(res, ims, -1.0)
        for tile in range(tiles):
            re, im = res[tile], ims[tile]
            if tile > 0:
                c, s = small[0, tile : tile + 1, :], small[1, tile : tile + 1, :]
                re, im = re * c + im * s, im * c - re * s
            at = group * tiles * GROUP + tile * GROUP + start % GROUP
            for part, lane in ((re, 0), (im, LANES)):
                part_high, part_low = split(part)
                high[at : at + CHUNK, lane : lane + LANES] = part_high
                low[at : at + CHUNK, lane : lane + LANES] = part_low
    at = slice(group * tiles * GROUP, (group + 1) * tiles * GROUP)
    return dot(
        jnp.concatenate([high[at, :], low[at, :], high[at, :]], axis=1),
        jnp.concatenate([forward[0], forward[0], forward[1]], axis=0),
    )


def transform(block, first, turn, small, forward, stage, high, low, spectrum, rows):
    tiles = block.shape[1] // LANES
    spread(block, first, stage)
    for group in range(rows // GROUP):
        at = slice(group * tiles * GROUP, (group + 1) * tiles * GROUP)
        spectrum[at, :] = forward_group(group, turn, small, forward, stage, high, low, rows, tiles)


def correlate(value, other):
    vr, vi = value[:, :LANES], value[:, LANES:]
    wr, wi = other[:, :LANES], other[:, LANES:]
    return jnp.concatenate([(vr * wr + vi * wi).astype(BF16), (vi * wr - vr * wi).astype(BF16)], axis=1)


def inverse_group(group, product, turn, small, inverse, back, gathered, rows, tiles):
    at = slice(group * tiles * GROUP, (group + 1) * tiles * GROUP)
    back[at, :] = dot(
        jnp.concatenate([product, product], axis=1),
        jnp.concatenate([inverse[0], inverse[1]], axis=0),
    )
    for start in range(group * GROUP, (group + 1) * GROUP, CHUNK):
        own = slice(start, start + CHUNK)
        res, ims = [], []
        for tile in range(tiles):
            row = group * tiles * GROUP + tile * GROUP + start % GROUP
            re = back[row : row + CHUNK, :LANES]
            im = back[row : row + CHUNK, LANES:]
            if tile > 0:
                c, s = small[0, tile : tile + 1, :], small[1, tile : tile + 1, :]
                re, im = re * c - im * s, im * c + re * s
            res.append(re)
            ims.append(im)
        res, ims = butterflies(res, ims, 1.0)
        for tile in range(tiles):
            lanes = slice(tile * LANES, (tile + 1) * LANES)
            c, s = turn[0, own, lanes], turn[1, own, lanes]
            re, im = res[tile], ims[tile]
            gathered[own, lanes] = (re * c - im * s).astype(BF16)
            gathered[rows + start : rows + start + CHUNK, lanes] = (im * c + re * s).astype(BF16)


def collapse(last, gathered):
    right = gathered[...]
    return dot(
        jnp.concatenate([last[0], last[1]], axis=1),
        jnp.concatenate([right, right], axis=0),
    )


def identity(size, dtype):
    row = lax.broadcasted_iota(jnp.int32, (size, size), 0)
    col = lax.broadcasted_iota(jnp.int32, (size, size), 1)
    return (row == col).astype(dtype)


def flipped(left, right):
    return lax.dot_general(left, right, (((1,), (1,)), ((), ())), preferred_element_type=F32)


def per_device_wide(inputs, cotangent, filter_taps, out_proj):
    devices = lax.axis_size("seq")
    groups = lax.axis_size("rep")
    chans = lax.axis_size("chan")
    tok_rows, chan_width = inputs.shape[1:]
    tiles = tok_rows // LANES
    narrow = chan_width // devices
    rows = chan_width
    first, last, turn, small, forward, inverse = (
        jnp.asarray(t) for t in tables(devices, 1, narrow, tok_rows)
    )
    shape = jax.ShapeDtypeStruct

    def call(kernel, out_shape, scratch=(), cost=3 * 10**6):
        return pl.pallas_call(
            kernel,
            out_shape=out_shape,
            scratch_shapes=scratch,
            compiler_params=pltpu.CompilerParams(vmem_limit_bytes=VMEM_LIMIT),
            cost_estimate=pl.CostEstimate(flops=10**8, bytes_accessed=cost, transcendentals=0),
        )

    def pieces(width):
        return (shape((devices, narrow, width), BF16),)

    def put(out_refs, source, lanes):
        out_refs[0][:, :, lanes] = source[...].reshape(devices, narrow, tok_rows).astype(BF16)

    def take(in_refs, lanes, block):
        block[...] = in_refs[0][:, :, lanes].astype(F32).reshape(rows, tok_rows).astype(BF16)

    def exchange(sent):
        return (lax.all_to_all(sent[0], "seq", split_axis=0, concat_axis=0, tiled=True),)

    count = 1
    front, behind = pl.ds(0, tok_rows), pl.ds(tok_rows, tok_rows)
    flat = pltpu.VMEM((rows, tok_rows), F32)
    block_scratch = pltpu.VMEM((rows, tok_rows), BF16)
    half_pair = [
        pltpu.VMEM((tiles * rows, 2 * LANES), BF16),
        pltpu.VMEM((tiles * rows, 2 * LANES), BF16),
    ]
    back_one = [pltpu.VMEM((2 * rows, tok_rows), BF16)]
    stage_scratch = pltpu.VMEM((2 * rows, tok_rows), F32)
    spec_shape = shape((tiles * rows, 2 * LANES), F32)
    spec_scratch = pltpu.VMEM((tiles * rows, 2 * LANES), F32)

    def pack_kernel(input_ref, taps_ref, *refs):
        *out_refs, wide = refs
        eye = identity(chan_width, BF16)
        wide[...] = flipped(eye, input_ref[...])
        put(out_refs, wide, front)
        wide[...] = flipped(eye, taps_ref[...])
        put(out_refs, wide, behind)

    def mix_kernel(own_ref, other_ref, proj_ref, *refs):
        *out_refs, wide = refs
        chan = lax.axis_index("chan")
        own = pl.ds(pl.multiple_of(chan * chan_width, chan_width), chan_width)
        other = pl.ds(pl.multiple_of((1 - chan) * chan_width, chan_width), chan_width)
        wide[...] = flipped(proj_ref[:, own], own_ref[...]) + flipped(proj_ref[:, other], other_ref[...])
        put(out_refs, wide, front)

    def early_kernel(*refs):
        recv, (first, turn, small, forward, input_ref, taps_ref, block, stage, high, low) = (
            refs[:count], refs[count:],
        )
        for lanes, spectrum in ((front, input_ref), (behind, taps_ref)):
            take(recv, lanes, block)
            transform(block[...], first, turn, small, forward, stage, high, low, spectrum, rows)

    count_groups = rows // GROUP

    def span(group):
        return slice(group * tiles * GROUP, (group + 1) * tiles * GROUP)

    def filter_kernel(*refs):
        recv, rest = refs[:count], refs[count:]
        (input_ref, first, last, turn, small, forward, inverse, grad, out_ref,
         block, stage, high, low, back, back_high) = rest
        take(recv, front, block)
        spread(block[...], first, stage)
        for group in range(count_groups):
            value = forward_group(group, turn, small, forward, stage, high, low, rows, tiles)
            grad[span(group), :] = value
            product = correlate(value, input_ref[span(group), :])
            inverse_group(group, product, turn, small, inverse, back, back_high, rows, tiles)
        out_ref[...] = collapse(last, back_high).astype(BF16)

    def input_kernel(grad, taps_ref, last, turn, small, inverse, *refs):
        *out_refs, back, back_high, wide = refs
        for group in range(count_groups):
            product = correlate(grad[span(group), :], taps_ref[span(group), :])
            inverse_group(group, product, turn, small, inverse, back, back_high, rows, tiles)
        wide[...] = collapse(last, back_high)
        put(out_refs, wide, front)

    def sum_kernel(own_ref, other_ref, *refs):
        *out_refs, wide = refs
        wide[...] = own_ref[...].astype(F32) + other_ref[...].astype(F32)
        put(out_refs, wide, front)

    def final_kernel(*refs):
        *recv, out_ref, block = refs
        take(recv, front, block)
        moved = lax.dot_general(
            block[...], identity(chan_width, BF16), (((0,), (0,)), ((), ())), preferred_element_type=F32
        )
        out_ref[...] = moved.astype(out_ref.dtype)

    own = cotangent.reshape(tok_rows, chan_width)
    other = lax.ppermute(own, "chan", [(k, (k + 1) % chans) for k in range(chans)])
    early = exchange(
        call(pack_kernel, pieces(2 * tok_rows), [flat])(inputs.reshape(tok_rows, chan_width), filter_taps)
    )
    late = exchange(call(mix_kernel, pieces(tok_rows), [flat])(own, other, out_proj))
    input_spec, taps_spec = call(
        early_kernel, (spec_shape, spec_shape), [block_scratch, stage_scratch] + half_pair, 9 * 10**6
    )(*early, first, turn, small, forward)
    grad_spec, partial = call(
        filter_kernel,
        (spec_shape, shape((rows, tok_rows), BF16)),
        [block_scratch, stage_scratch] + half_pair + [spec_scratch] + back_one,
        9 * 10**6,
    )(*late, input_spec, first, last, turn, small, forward, inverse)
    partial_other = lax.ppermute(partial, "rep", [(k, (k + 1) % groups) for k in range(groups)])
    input_back = exchange(
        call(input_kernel, pieces(tok_rows), [spec_scratch] + back_one + [flat], 6 * 10**6)(
            grad_spec, taps_spec, last, turn, small, inverse
        )
    )
    filter_back = exchange(call(sum_kernel, pieces(tok_rows), [flat])(partial, partial_other))
    grad_input = call(final_kernel, shape((tok_rows, chan_width), BF16), [block_scratch])(*input_back)
    grad_filter = call(final_kernel, shape((tok_rows, chan_width), F32), [block_scratch])(*filter_back)
    return grad_input.reshape(1, tok_rows, chan_width), grad_filter


def per_device_near(inputs, cotangent, filter_taps, out_proj):
    devices = lax.axis_size("seq")
    groups = lax.axis_size("rep")
    tok_rows, chan_width = inputs.shape[1:]
    tiles = tok_rows // LANES
    narrow = chan_width // devices
    rows = chan_width
    chips = devices // CORES
    wide_rows = CORES * narrow
    half = chips * narrow
    first, last, turn, small, forward, inverse = (
        jnp.asarray(t) for t in tables(devices, 1, narrow, tok_rows)
    )
    shape = jax.ShapeDtypeStruct
    swap_pairs = [(k, k ^ 1) for k in range(devices)]

    def call(kernel, out_shape, scratch=(), cost=3 * 10**6):
        return pl.pallas_call(
            kernel,
            out_shape=out_shape,
            scratch_shapes=scratch,
            compiler_params=pltpu.CompilerParams(vmem_limit_bytes=VMEM_LIMIT),
            cost_estimate=pl.CostEstimate(flops=10**8, bytes_accessed=cost, transcendentals=0),
        )

    def swap(value):
        return lax.ppermute(value, "seq", swap_pairs)

    def cross(value, axis):
        size = lax.axis_size(axis)
        return lax.ppermute(value, axis, [(k, (k + 1) % size) for k in range(size)])

    def exchange(sent):
        got = [sent[0]]
        for offset in range(1, chips):
            pairs = [(k, k ^ (offset * CORES)) for k in range(devices)]
            got.append(lax.ppermute(sent[offset], "seq", pairs))
        return tuple(got)

    def place():
        at = lax.axis_index("seq")
        return at // CORES, at % CORES

    def pieces(width):
        return tuple(shape((CORES, narrow, width), BF16) for _ in range(chips))

    part_rows = tok_rows // groups
    front, behind = pl.ds(0, tok_rows), pl.ds(tok_rows, part_rows)
    block_scratch = pltpu.VMEM((rows, tok_rows), BF16)
    half_pair = [
        pltpu.VMEM((tiles * rows, 2 * LANES), BF16),
        pltpu.VMEM((tiles * rows, 2 * LANES), BF16),
    ]
    back_one = [pltpu.VMEM((2 * rows, tok_rows), BF16)]
    stage_scratch = pltpu.VMEM((2 * rows, tok_rows), F32)
    spec_shape = shape((tiles * rows, 2 * LANES), F32)
    spec_scratch = pltpu.VMEM((tiles * rows, 2 * LANES), F32)
    flat = pltpu.VMEM((rows, tok_rows), F32)
    half_scratch = pltpu.VMEM((half, tok_rows), F32)
    halves = (shape((chips, narrow, tok_rows), BF16), shape((chips, narrow, tok_rows), BF16))

    def put(out_refs, source, side, lanes, part=slice(None)):
        chip, _ = place()
        for offset in range(chips):
            at = pl.multiple_of((chip ^ offset) * narrow, narrow)
            out_refs[offset][pl.ds(side, 1), :, lanes] = (
                source[pl.ds(at, narrow), part][None].astype(BF16)
            )

    def take(in_refs, lanes, block):
        chip, _ = place()
        for offset in range(chips):
            at = pl.multiple_of((chip ^ offset) * wide_rows, wide_rows)
            for core in range(CORES):
                block[pl.ds(at + core * narrow, narrow), :] = in_refs[offset][core, :, lanes]

    def cut(source, mine_ref, theirs_ref):
        _, core = place()
        for chip in range(chips):
            for ref, side in ((mine_ref, core), (theirs_ref, 1 - core)):
                at = pl.multiple_of(chip * wide_rows + side * narrow, narrow)
                ref[chip] = source[pl.ds(at, narrow), :].astype(BF16)

    def chosen(core):
        row = lax.broadcasted_iota(jnp.int32, (half, chan_width), 0)
        col = lax.broadcasted_iota(jnp.int32, (half, chan_width), 1)
        pick = (row // narrow) * wide_rows + core * narrow + row % narrow
        return (pick == col).astype(F32).astype(BF16)

    def pack_kernel(held_ref, input_near, taps_near, *refs):
        *out_refs, wide = refs
        _, core = place()
        pick = chosen(core)
        start = pl.multiple_of(lax.axis_index("rep") * part_rows, part_rows)
        wide[...] = flipped(pick, held_ref[:tok_rows, :])
        put(out_refs, wide, core, front)
        wide[...] = flipped(pick, input_near[...])
        put(out_refs, wide, 1 - core, front)
        part = pl.ds(0, part_rows)
        wide[:, part] = flipped(pick, held_ref[tok_rows:, :])
        put(out_refs, wide, core, behind, part)
        wide[:, part] = flipped(pick, taps_near[pl.ds(start, part_rows), :])
        put(out_refs, wide, 1 - core, behind, part)

    def taps_kernel(gate_ref, *refs):
        *recv, out_ref = refs
        take(recv, behind, out_ref)

    def own_kernel(own_ref, proj_ref, near_ref, part_ref, part_near, other_ref):
        chan = lax.axis_index("chan")
        _, core = place()
        picked = [
            proj_ref[pl.ds(pl.multiple_of(chip * wide_rows + core * narrow, narrow), narrow), :]
            for chip in range(chips)
        ]
        held = jnp.concatenate(picked, axis=0)
        swapped = jnp.concatenate([held[:, chan_width:], held[:, :chan_width]], axis=1)
        held = jnp.where(chan == 0, held, swapped)
        part_ref[...] = flipped(held[:, :chan_width], own_ref[...])
        part_near[...] = flipped(held[:, :chan_width], near_ref[...])
        other_ref[...] = held[:, chan_width:]

    def mix_kernel(part_ref, part_near, proj_ref, other_ref, other_near, *refs):
        *out_refs, wide = refs
        _, core = place()
        for part, ref, side in ((part_ref, other_ref, core), (part_near, other_near, 1 - core)):
            wide[...] = part[...] + flipped(proj_ref[...], ref[...])
            put(out_refs, wide, side, front)

    def signal_kernel(*refs):
        recv, (first, turn, small, forward, spectrum, block, stage, high, low) = refs[:chips], refs[chips:]
        take(recv, front, block)
        transform(block[...], first, turn, small, forward, stage, high, low, spectrum, rows)

    def taps_spec_kernel(own_ref, other_ref, first, turn, small, forward, spectrum, block, stage, high, low):
        index = lax.axis_index("rep")
        for ref, at in ((own_ref, index), (other_ref, 1 - index)):
            block[:, pl.ds(pl.multiple_of(at * part_rows, part_rows), part_rows)] = ref[...]
        transform(block[...], first, turn, small, forward, stage, high, low, spectrum, rows)

    count_groups = rows // GROUP

    def span(group):
        return slice(group * tiles * GROUP, (group + 1) * tiles * GROUP)

    def filter_kernel(*refs):
        recv, rest = refs[:chips], refs[chips:]
        (input_ref, first, last, turn, small, forward, inverse, grad, mine_ref, theirs_ref,
         block, stage, high, low, back, back_high, wide) = rest
        take(recv, front, block)
        spread(block[...], first, stage)
        for group in range(count_groups):
            value = forward_group(group, turn, small, forward, stage, high, low, rows, tiles)
            grad[span(group), :] = value
            product = correlate(value, input_ref[span(group), :])
            inverse_group(group, product, turn, small, inverse, back, back_high, rows, tiles)
        wide[...] = collapse(last, back_high)
        cut(wide, mine_ref, theirs_ref)

    def input_kernel(grad, taps_ref, last, turn, small, inverse, *refs):
        *out_refs, back, back_high, wide = refs
        for group in range(count_groups):
            product = correlate(grad[span(group), :], taps_ref[span(group), :])
            inverse_group(group, product, turn, small, inverse, back, back_high, rows, tiles)
        wide[...] = collapse(last, back_high)
        chip, _ = place()
        for offset in range(chips):
            at = pl.multiple_of((chip ^ offset) * wide_rows, wide_rows)
            out_refs[offset][...] = (
                wide[pl.ds(at, wide_rows), :].reshape(CORES, narrow, tok_rows).astype(BF16)
            )

    def gate_kernel(value_ref, out_ref):
        out_ref[...] = value_ref[:16, :]

    def sum_kernel(mine_ref, mine_other, near_ref, near_other, *out_refs):
        chip, core = place()
        for offset in range(chips):
            at = pl.ds(chip ^ offset, 1)
            for ref, other, side in ((mine_ref, mine_other, core), (near_ref, near_other, 1 - core)):
                total = ref[at].astype(F32) + other[at].astype(F32)
                out_refs[offset][pl.ds(side, 1)] = total.astype(BF16)

    def final_kernel(*refs):
        *recv, out_ref, block = refs
        if len(recv) == chips:
            take(recv, front, block)
        else:
            chip, core = place()
            for offset in range(chips):
                for flip in range(CORES):
                    at = pl.multiple_of((chip ^ offset) * wide_rows + (core ^ flip) * narrow, narrow)
                    block[pl.ds(at, narrow), :] = recv[flip * chips + offset][core]
        moved = lax.dot_general(
            block[...], identity(chan_width, BF16), (((0,), (0,)), ((), ())), preferred_element_type=F32
        )
        out_ref[...] = moved.astype(out_ref.dtype)

    signal = inputs.reshape(tok_rows, chan_width)
    own = cotangent.reshape(tok_rows, chan_width)
    signal_near = swap(signal)
    taps_near = swap(filter_taps)
    other = cross(own, "chan")
    own_near = swap(own)
    taps_part = lax.dynamic_slice_in_dim(filter_taps, lax.axis_index("rep") * part_rows, part_rows, 0)
    held = jnp.concatenate([signal, taps_part], axis=0)
    early = exchange(
        call(
            pack_kernel,
            pieces(tok_rows + part_rows),
            [half_scratch],
        )(held, signal_near, taps_near),
    )
    part_shape = shape((half, tok_rows), F32)
    part, part_near, proj_other = call(
        own_kernel,
        (part_shape, part_shape, shape((half, chan_width), BF16)),
    )(own, out_proj, own_near)
    other_near = swap(other)
    late = exchange(call(mix_kernel, pieces(tok_rows), [half_scratch])(part, part_near, proj_other, other, other_near))
    gate = call(gate_kernel, shape((16, chan_width), BF16), (), 10**4)(proj_other)
    own_taps = call(taps_kernel, shape((rows, part_rows), BF16))(gate, *early)
    other_taps = cross(own_taps, "rep")
    transform_scratch = [block_scratch, stage_scratch] + half_pair
    input_spec = call(signal_kernel, spec_shape, transform_scratch, 6 * 10**6)(
        *early, first, turn, small, forward
    )
    grad_spec, mine, theirs = call(
        filter_kernel,
        (spec_shape,) + halves,
        [block_scratch, stage_scratch] + half_pair + [spec_scratch] + back_one + [flat],
        12 * 10**6,
    )(*late, input_spec, first, last, turn, small, forward, inverse)
    mine_other = cross(mine, "rep")
    near = swap(theirs)
    near_other = cross(near, "rep")
    taps_spec = call(taps_spec_kernel, spec_shape, transform_scratch, 6 * 10**6)(
        own_taps, other_taps, first, turn, small, forward
    )
    input_sent = call(
        input_kernel, pieces(tok_rows), [spec_scratch] + back_one + [flat], 6 * 10**6
    )(grad_spec, taps_spec, last, turn, small, inverse)
    input_back = exchange(input_sent)
    input_back += tuple(swap(piece) for piece in input_back)
    filter_back = exchange(call(sum_kernel, pieces(tok_rows))(mine, mine_other, near, near_other))
    grad_input = call(final_kernel, shape((tok_rows, chan_width), BF16), [block_scratch])(*input_back)
    grad_filter = call(final_kernel, shape((tok_rows, chan_width), F32), [block_scratch])(*filter_back)
    return grad_input.reshape(1, tok_rows, chan_width), grad_filter


def solution(mesh):
    few = mesh.shape["seq"] == CORES * MAX_DIRECT
    body = per_device_near if few else per_device_wide

    return jax.shard_map(
        body,
        mesh=mesh,
        in_specs=(
            P("rep", "seq", "chan"),
            P("rep", "seq", "chan"),
            P("seq", "chan"),
            P("chan", None),
        ),
        out_specs=(P("rep", "seq", "chan"), P("seq", "chan")),
        check_vma=False,
    )
```

```python
import math

import jax
import jax.numpy as jnp
import numpy as np
from jax import lax
from jax.experimental import pallas as pl
from jax.experimental.pallas import tpu as pltpu
from jax.sharding import PartitionSpec as P


LANES = 128
F32 = jnp.float32
BF16 = jnp.bfloat16
VMEM_LIMIT = 48 * 1024 * 1024
CORES = 2
MAX_DIRECT = 4


def split(values):
    high = values.astype(BF16)
    low = (values - high.astype(F32)).astype(BF16)
    return high, low


def split_table(table):
    table = np.asarray(table, np.float32)
    high = table.astype(BF16)
    low = (table - high.astype(np.float32)).astype(BF16)
    return np.stack([high, low])


def phase(numerator, modulus):
    angle = 2.0 * math.pi * np.mod(numerator, modulus) / modulus
    return np.cos(angle), np.sin(angle)


def tables(devices, groups, narrow, tok_rows):
    length = devices * tok_rows
    tiles = tok_rows // LANES
    rows = groups * devices * narrow
    dev = np.arange(devices)
    quarter = 4 * dev + 1
    cos_d, sin_d = phase(quarter[:, None] * dev[None, :], 4 * devices)
    eye_g, eye_c = np.eye(groups), np.eye(narrow)

    def expand(square):
        return np.einsum("gh,jd,ce->gjchde", eye_g, square, eye_c).reshape(rows, rows)

    cos_d, sin_d = expand(cos_d), expand(sin_d)
    first = split_table(np.concatenate([cos_d, -sin_d], axis=0))
    last = split_table(np.concatenate([cos_d.T, -sin_d.T], axis=1) / length)
    local = np.arange(tok_rows)
    cos_r, sin_r = phase(quarter[:, None] * local[None, :], 4 * length)

    def widen(block):
        block = np.broadcast_to(block[None, :, None, :], (groups, devices, narrow, tok_rows))
        return block.reshape(rows, tok_rows)

    turn = np.stack([widen(cos_r), widen(sin_r)]).astype(np.float32)
    lane = np.arange(LANES)
    step = np.arange(tiles)
    cos_s, sin_s = phase(step[:, None] * lane[None, :], tok_rows)
    small = np.stack([cos_s, sin_s]).astype(np.float32)
    cos_b, sin_b = phase(lane[:, None] * lane[None, :], LANES)
    forward = split_table(np.block([[cos_b, -sin_b], [sin_b, cos_b]]))
    inverse = split_table(np.block([[cos_b, sin_b], [-sin_b, cos_b]]))
    return first, last, turn, small, forward, inverse


def butterflies(real_parts, imag_parts, sign):
    size = len(real_parts)
    if size == 1:
        return real_parts, imag_parts
    even_re, even_im = butterflies(real_parts[0::2], imag_parts[0::2], sign)
    odd_re, odd_im = butterflies(real_parts[1::2], imag_parts[1::2], sign)
    low_re, low_im, high_re, high_im = [], [], [], []
    for index in range(size // 2):
        re, im = odd_re[index], odd_im[index]
        if index == 0:
            turned = (re, im)
        elif 4 * index == size:
            turned = (-im, re) if sign > 0 else (im, -re)
        else:
            angle = sign * 2.0 * math.pi * index / size
            c, s = math.cos(angle), math.sin(angle)
            if 8 * index == size:
                turned = ((re - im) * c, (re + im) * c) if sign > 0 else ((re + im) * c, (im - re) * c)
            else:
                turned = (re * c - im * s, re * s + im * c)
        low_re.append(even_re[index] + turned[0])
        low_im.append(even_im[index] + turned[1])
        high_re.append(even_re[index] - turned[0])
        high_im.append(even_im[index] - turned[1])
    return low_re + high_re, low_im + high_im


def dot(lhs, rhs):
    return jnp.dot(lhs, rhs, preferred_element_type=F32)


CHUNK = 8
GROUP = 32


def spread(block, first, stage):
    table = jnp.concatenate([first[0], first[1]], axis=1)
    stage[...] = dot(table, jnp.concatenate([block, block], axis=0))


def forward_group(group, turn, small, forward, stage, high, low, rows, tiles):
    for start in range(group * GROUP, (group + 1) * GROUP, CHUNK):
        own = slice(start, start + CHUNK)
        res, ims = [], []
        for tile in range(tiles):
            lanes = slice(tile * LANES, (tile + 1) * LANES)
            re = stage[own, lanes]
            im = stage[rows + start : rows + start + CHUNK, lanes]
            c, s = turn[0, own, lanes], turn[1, own, lanes]
            res.append(re * c + im * s)
            ims.append(im * c - re * s)
        res, ims = butterflies(res, ims, -1.0)
        for tile in range(tiles):
            re, im = res[tile], ims[tile]
            if tile > 0:
                c, s = small[0, tile : tile + 1, :], small[1, tile : tile + 1, :]
                re, im = re * c + im * s, im * c - re * s
            at = group * tiles * GROUP + tile * GROUP + start % GROUP
            for part, lane in ((re, 0), (im, LANES)):
                part_high, part_low = split(part)
                high[at : at + CHUNK, lane : lane + LANES] = part_high
                low[at : at + CHUNK, lane : lane + LANES] = part_low
    at = slice(group * tiles * GROUP, (group + 1) * tiles * GROUP)
    return dot(
        jnp.concatenate([high[at, :], low[at, :], high[at, :]], axis=1),
        jnp.concatenate([forward[0], forward[0], forward[1]], axis=0),
    )


def transform(block, first, turn, small, forward, stage, high, low, spectrum, rows):
    tiles = block.shape[1] // LANES
    spread(block, first, stage)
    for group in range(rows // GROUP):
        at = slice(group * tiles * GROUP, (group + 1) * tiles * GROUP)
        spectrum[at, :] = forward_group(group, turn, small, forward, stage, high, low, rows, tiles)


def correlate(value, other):
    vr, vi = value[:, :LANES], value[:, LANES:]
    wr, wi = other[:, :LANES], other[:, LANES:]
    return jnp.concatenate([(vr * wr + vi * wi).astype(BF16), (vi * wr - vr * wi).astype(BF16)], axis=1)


def inverse_group(group, product, turn, small, inverse, back, gathered, rows, tiles):
    at = slice(group * tiles * GROUP, (group + 1) * tiles * GROUP)
    back[at, :] = dot(
        jnp.concatenate([product, product], axis=1),
        jnp.concatenate([inverse[0], inverse[1]], axis=0),
    )
    for start in range(group * GROUP, (group + 1) * GROUP, CHUNK):
        own = slice(start, start + CHUNK)
        res, ims = [], []
        for tile in range(tiles):
            row = group * tiles * GROUP + tile * GROUP + start % GROUP
            re = back[row : row + CHUNK, :LANES]
            im = back[row : row + CHUNK, LANES:]
            if tile > 0:
                c, s = small[0, tile : tile + 1, :], small[1, tile : tile + 1, :]
                re, im = re * c - im * s, im * c + re * s
            res.append(re)
            ims.append(im)
        res, ims = butterflies(res, ims, 1.0)
        for tile in range(tiles):
            lanes = slice(tile * LANES, (tile + 1) * LANES)
            c, s = turn[0, own, lanes], turn[1, own, lanes]
            re, im = res[tile], ims[tile]
            gathered[own, lanes] = (re * c - im * s).astype(BF16)
            gathered[rows + start : rows + start + CHUNK, lanes] = (im * c + re * s).astype(BF16)


def collapse(last, gathered):
    right = gathered[...]
    return dot(
        jnp.concatenate([last[0], last[1]], axis=1),
        jnp.concatenate([right, right], axis=0),
    )


def identity(size, dtype):
    row = lax.broadcasted_iota(jnp.int32, (size, size), 0)
    col = lax.broadcasted_iota(jnp.int32, (size, size), 1)
    return (row == col).astype(dtype)


def flipped(left, right):
    return lax.dot_general(left, right, (((1,), (1,)), ((), ())), preferred_element_type=F32)


def per_device_wide(inputs, cotangent, filter_taps, out_proj):
    devices = lax.axis_size("seq")
    groups = lax.axis_size("rep")
    chans = lax.axis_size("chan")
    tok_rows, chan_width = inputs.shape[1:]
    tiles = tok_rows // LANES
    narrow = chan_width // devices
    rows = chan_width
    first, last, turn, small, forward, inverse = (
        jnp.asarray(t) for t in tables(devices, 1, narrow, tok_rows)
    )
    shape = jax.ShapeDtypeStruct

    def call(kernel, out_shape, scratch=(), cost=3 * 10**6):
        return pl.pallas_call(
            kernel,
            out_shape=out_shape,
            scratch_shapes=scratch,
            compiler_params=pltpu.CompilerParams(vmem_limit_bytes=VMEM_LIMIT),
            cost_estimate=pl.CostEstimate(flops=10**8, bytes_accessed=cost, transcendentals=0),
        )

    def pieces(width):
        return (shape((devices, narrow, width), BF16),)

    def put(out_refs, source, lanes):
        out_refs[0][:, :, lanes] = source[...].reshape(devices, narrow, tok_rows).astype(BF16)

    def take(in_refs, lanes, block):
        block[...] = in_refs[0][:, :, lanes].astype(F32).reshape(rows, tok_rows).astype(BF16)

    def exchange(sent):
        return (lax.all_to_all(sent[0], "seq", split_axis=0, concat_axis=0, tiled=True),)

    count = 1
    front, behind = pl.ds(0, tok_rows), pl.ds(tok_rows, tok_rows)
    flat = pltpu.VMEM((rows, tok_rows), F32)
    block_scratch = pltpu.VMEM((rows, tok_rows), BF16)
    half_pair = [
        pltpu.VMEM((tiles * rows, 2 * LANES), BF16),
        pltpu.VMEM((tiles * rows, 2 * LANES), BF16),
    ]
    back_one = [pltpu.VMEM((2 * rows, tok_rows), BF16)]
    stage_scratch = pltpu.VMEM((2 * rows, tok_rows), F32)
    spec_shape = shape((tiles * rows, 2 * LANES), F32)
    spec_scratch = pltpu.VMEM((tiles * rows, 2 * LANES), F32)

    def pack_kernel(input_ref, taps_ref, *refs):
        *out_refs, wide = refs
        eye = identity(chan_width, BF16)
        wide[...] = flipped(eye, input_ref[...])
        put(out_refs, wide, front)
        wide[...] = flipped(eye, taps_ref[...])
        put(out_refs, wide, behind)

    def mix_kernel(own_ref, other_ref, proj_ref, *refs):
        *out_refs, wide = refs
        chan = lax.axis_index("chan")
        own = pl.ds(pl.multiple_of(chan * chan_width, chan_width), chan_width)
        other = pl.ds(pl.multiple_of((1 - chan) * chan_width, chan_width), chan_width)
        wide[...] = flipped(proj_ref[:, own], own_ref[...]) + flipped(proj_ref[:, other], other_ref[...])
        put(out_refs, wide, front)

    def early_kernel(*refs):
        recv, (first, turn, small, forward, input_ref, taps_ref, block, stage, high, low) = (
            refs[:count], refs[count:],
        )
        for lanes, spectrum in ((front, input_ref), (behind, taps_ref)):
            take(recv, lanes, block)
            transform(block[...], first, turn, small, forward, stage, high, low, spectrum, rows)

    count_groups = rows // GROUP

    def span(group):
        return slice(group * tiles * GROUP, (group + 1) * tiles * GROUP)

    def filter_kernel(*refs):
        recv, rest = refs[:count], refs[count:]
        (input_ref, first, last, turn, small, forward, inverse, grad, out_ref,
         block, stage, high, low, back, back_high) = rest
        take(recv, front, block)
        spread(block[...], first, stage)
        for group in range(count_groups):
            value = forward_group(group, turn, small, forward, stage, high, low, rows, tiles)
            grad[span(group), :] = value
            product = correlate(value, input_ref[span(group), :])
            inverse_group(group, product, turn, small, inverse, back, back_high, rows, tiles)
        out_ref[...] = collapse(last, back_high).astype(BF16)

    def input_kernel(grad, taps_ref, last, turn, small, inverse, *refs):
        *out_refs, back, back_high, wide = refs
        for group in range(count_groups):
            product = correlate(grad[span(group), :], taps_ref[span(group), :])
            inverse_group(group, product, turn, small, inverse, back, back_high, rows, tiles)
        wide[...] = collapse(last, back_high)
        put(out_refs, wide, front)

    def sum_kernel(own_ref, other_ref, *refs):
        *out_refs, wide = refs
        wide[...] = own_ref[...].astype(F32) + other_ref[...].astype(F32)
        put(out_refs, wide, front)

    def final_kernel(*refs):
        *recv, out_ref, block = refs
        take(recv, front, block)
        moved = lax.dot_general(
            block[...], identity(chan_width, BF16), (((0,), (0,)), ((), ())), preferred_element_type=F32
        )
        out_ref[...] = moved.astype(out_ref.dtype)

    own = cotangent.reshape(tok_rows, chan_width)
    other = lax.ppermute(own, "chan", [(k, (k + 1) % chans) for k in range(chans)])
    early = exchange(
        call(pack_kernel, pieces(2 * tok_rows), [flat])(inputs.reshape(tok_rows, chan_width), filter_taps)
    )
    late = exchange(call(mix_kernel, pieces(tok_rows), [flat])(own, other, out_proj))
    input_spec, taps_spec = call(
        early_kernel, (spec_shape, spec_shape), [block_scratch, stage_scratch] + half_pair, 9 * 10**6
    )(*early, first, turn, small, forward)
    grad_spec, partial = call(
        filter_kernel,
        (spec_shape, shape((rows, tok_rows), BF16)),
        [block_scratch, stage_scratch] + half_pair + [spec_scratch] + back_one,
        9 * 10**6,
    )(*late, input_spec, first, last, turn, small, forward, inverse)
    partial_other = lax.ppermute(partial, "rep", [(k, (k + 1) % groups) for k in range(groups)])
    input_back = exchange(
        call(input_kernel, pieces(tok_rows), [spec_scratch] + back_one + [flat], 6 * 10**6)(
            grad_spec, taps_spec, last, turn, small, inverse
        )
    )
    filter_back = exchange(call(sum_kernel, pieces(tok_rows), [flat])(partial, partial_other))
    grad_input = call(final_kernel, shape((tok_rows, chan_width), BF16), [block_scratch])(*input_back)
    grad_filter = call(final_kernel, shape((tok_rows, chan_width), F32), [block_scratch])(*filter_back)
    return grad_input.reshape(1, tok_rows, chan_width), grad_filter


def per_device_near(inputs, cotangent, filter_taps, out_proj):
    devices = lax.axis_size("seq")
    groups = lax.axis_size("rep")
    tok_rows, chan_width = inputs.shape[1:]
    tiles = tok_rows // LANES
    narrow = chan_width // devices
    rows = chan_width
    chips = devices // CORES
    wide_rows = CORES * narrow
    half = chips * narrow
    first, last, turn, small, forward, inverse = (
        jnp.asarray(t) for t in tables(devices, 1, narrow, tok_rows)
    )
    shape = jax.ShapeDtypeStruct
    swap_pairs = [(k, k ^ 1) for k in range(devices)]

    def call(kernel, out_shape, scratch=(), cost=3 * 10**6):
        return pl.pallas_call(
            kernel,
            out_shape=out_shape,
            scratch_shapes=scratch,
            compiler_params=pltpu.CompilerParams(vmem_limit_bytes=VMEM_LIMIT),
            cost_estimate=pl.CostEstimate(flops=10**8, bytes_accessed=cost, transcendentals=0),
        )

    def swap(value):
        return lax.ppermute(value, "seq", swap_pairs)

    def cross(value, axis):
        size = lax.axis_size(axis)
        return lax.ppermute(value, axis, [(k, (k + 1) % size) for k in range(size)])

    def exchange(sent):
        got = [sent[0]]
        for offset in range(1, chips):
            pairs = [(k, k ^ (offset * CORES)) for k in range(devices)]
            got.append(lax.ppermute(sent[offset], "seq", pairs))
        return tuple(got)

    def place():
        at = lax.axis_index("seq")
        return at // CORES, at % CORES

    def pieces(width):
        return tuple(shape((CORES, narrow, width), BF16) for _ in range(chips))

    part_rows = tok_rows // groups
    front, behind = pl.ds(0, tok_rows), pl.ds(tok_rows, part_rows)
    block_scratch = pltpu.VMEM((rows, tok_rows), BF16)
    half_pair = [
        pltpu.VMEM((tiles * rows, 2 * LANES), BF16),
        pltpu.VMEM((tiles * rows, 2 * LANES), BF16),
    ]
    back_one = [pltpu.VMEM((2 * rows, tok_rows), BF16)]
    stage_scratch = pltpu.VMEM((2 * rows, tok_rows), F32)
    spec_shape = shape((tiles * rows, 2 * LANES), F32)
    spec_scratch = pltpu.VMEM((tiles * rows, 2 * LANES), F32)
    flat = pltpu.VMEM((rows, tok_rows), F32)
    half_scratch = pltpu.VMEM((half, tok_rows), F32)
    halves = (shape((chips, narrow, tok_rows), BF16), shape((chips, narrow, tok_rows), BF16))

    def put(out_refs, source, side, lanes, part=slice(None)):
        chip, _ = place()
        for offset in range(chips):
            at = pl.multiple_of((chip ^ offset) * narrow, narrow)
            out_refs[offset][pl.ds(side, 1), :, lanes] = (
                source[pl.ds(at, narrow), part][None].astype(BF16)
            )

    def take(in_refs, lanes, block):
        chip, _ = place()
        for offset in range(chips):
            at = pl.multiple_of((chip ^ offset) * wide_rows, wide_rows)
            for core in range(CORES):
                block[pl.ds(at + core * narrow, narrow), :] = in_refs[offset][core, :, lanes]

    def cut(source, mine_ref, theirs_ref):
        _, core = place()
        for chip in range(chips):
            for ref, side in ((mine_ref, core), (theirs_ref, 1 - core)):
                at = pl.multiple_of(chip * wide_rows + side * narrow, narrow)
                ref[chip] = source[pl.ds(at, narrow), :].astype(BF16)

    def chosen(core):
        row = lax.broadcasted_iota(jnp.int32, (half, chan_width), 0)
        col = lax.broadcasted_iota(jnp.int32, (half, chan_width), 1)
        pick = (row // narrow) * wide_rows + core * narrow + row % narrow
        return (pick == col).astype(F32).astype(BF16)

    def pack_kernel(input_ref, taps_ref, input_near, taps_near, *refs):
        *out_refs, wide = refs
        _, core = place()
        pick = chosen(core)
        part = pl.ds(0, part_rows)
        for own_ref, near_ref, lanes, span_in in (
            (input_ref, input_near, front, slice(None)), (taps_ref, taps_near, behind, part),
        ):
            for ref, side in ((own_ref, core), (near_ref, 1 - core)):
                wide[:, span_in] = flipped(pick, ref[...])
                put(out_refs, wide, side, lanes, span_in)

    def taps_kernel(gate_ref, *refs):
        *recv, out_ref = refs
        take(recv, behind, out_ref)

    def own_kernel(own_ref, proj_ref, near_ref, part_ref, part_near, other_ref):
        chan = lax.axis_index("chan")
        _, core = place()
        picked = [
            proj_ref[pl.ds(pl.multiple_of(chip * wide_rows + core * narrow, narrow), narrow), :]
            for chip in range(chips)
        ]
        held = jnp.concatenate(picked, axis=0)
        swapped = jnp.concatenate([held[:, chan_width:], held[:, :chan_width]], axis=1)
        held = jnp.where(chan == 0, held, swapped)
        part_ref[...] = flipped(held[:, :chan_width], own_ref[...])
        part_near[...] = flipped(held[:, :chan_width], near_ref[...])
        other_ref[...] = held[:, chan_width:]

    def mix_kernel(part_ref, part_near, proj_ref, other_ref, other_near, *refs):
        *out_refs, wide = refs
        _, core = place()
        for part, ref, side in ((part_ref, other_ref, core), (part_near, other_near, 1 - core)):
            wide[...] = part[...] + flipped(proj_ref[...], ref[...])
            put(out_refs, wide, side, front)

    def signal_kernel(*refs):
        recv, (first, turn, small, forward, spectrum, block, stage, high, low) = refs[:chips], refs[chips:]
        take(recv, front, block)
        transform(block[...], first, turn, small, forward, stage, high, low, spectrum, rows)

    def taps_spec_kernel(own_ref, other_ref, first, turn, small, forward, spectrum, block, stage, high, low):
        index = lax.axis_index("rep")
        for ref, at in ((own_ref, index), (other_ref, 1 - index)):
            block[:, pl.ds(pl.multiple_of(at * part_rows, part_rows), part_rows)] = ref[...]
        transform(block[...], first, turn, small, forward, stage, high, low, spectrum, rows)

    count_groups = rows // GROUP

    def span(group):
        return slice(group * tiles * GROUP, (group + 1) * tiles * GROUP)

    def filter_kernel(*refs):
        recv, rest = refs[:chips], refs[chips:]
        (input_ref, first, last, turn, small, forward, inverse, grad, mine_ref, theirs_ref,
         block, stage, high, low, back, back_high, wide) = rest
        take(recv, front, block)
        spread(block[...], first, stage)
        for group in range(count_groups):
            value = forward_group(group, turn, small, forward, stage, high, low, rows, tiles)
            grad[span(group), :] = value
            product = correlate(value, input_ref[span(group), :])
            inverse_group(group, product, turn, small, inverse, back, back_high, rows, tiles)
        wide[...] = collapse(last, back_high)
        cut(wide, mine_ref, theirs_ref)

    def input_kernel(grad, taps_ref, last, turn, small, inverse, *refs):
        *out_refs, back, back_high, wide = refs
        for group in range(count_groups):
            product = correlate(grad[span(group), :], taps_ref[span(group), :])
            inverse_group(group, product, turn, small, inverse, back, back_high, rows, tiles)
        wide[...] = collapse(last, back_high)
        chip, _ = place()
        for offset in range(chips):
            at = pl.multiple_of((chip ^ offset) * wide_rows, wide_rows)
            out_refs[offset][...] = (
                wide[pl.ds(at, wide_rows), :].reshape(CORES, narrow, tok_rows).astype(BF16)
            )

    def gate_kernel(value_ref, out_ref):
        out_ref[...] = value_ref[:16, :]

    def sum_kernel(mine_ref, mine_other, near_ref, near_other, *out_refs):
        chip, core = place()
        for offset in range(chips):
            at = pl.ds(chip ^ offset, 1)
            for ref, other, side in ((mine_ref, mine_other, core), (near_ref, near_other, 1 - core)):
                total = ref[at].astype(F32) + other[at].astype(F32)
                out_refs[offset][pl.ds(side, 1)] = total.astype(BF16)

    def final_kernel(*refs):
        *recv, out_ref, block = refs
        if len(recv) == chips:
            take(recv, front, block)
        else:
            chip, core = place()
            for offset in range(chips):
                for flip in range(CORES):
                    at = pl.multiple_of((chip ^ offset) * wide_rows + (core ^ flip) * narrow, narrow)
                    block[pl.ds(at, narrow), :] = recv[flip * chips + offset][core]
        moved = lax.dot_general(
            block[...], identity(chan_width, BF16), (((0,), (0,)), ((), ())), preferred_element_type=F32
        )
        out_ref[...] = moved.astype(out_ref.dtype)

    signal = inputs.reshape(tok_rows, chan_width)
    own = cotangent.reshape(tok_rows, chan_width)
    signal_near = swap(signal)
    taps_part = lax.dynamic_slice_in_dim(filter_taps, lax.axis_index("rep") * part_rows, part_rows, 0)
    taps_near = swap(taps_part)
    other = cross(own, "chan")
    own_near = swap(own)
    early = exchange(
        call(
            pack_kernel,
            pieces(tok_rows + part_rows),
            [half_scratch],
        )(signal, taps_part, signal_near, taps_near),
    )
    part_shape = shape((half, tok_rows), F32)
    part, part_near, proj_other = call(
        own_kernel,
        (part_shape, part_shape, shape((half, chan_width), BF16)),
    )(own, out_proj, own_near)
    other_near = swap(other)
    late = exchange(call(mix_kernel, pieces(tok_rows), [half_scratch])(part, part_near, proj_other, other, other_near))
    gate = call(gate_kernel, shape((16, chan_width), BF16), (), 10**4)(proj_other)
    own_taps = call(taps_kernel, shape((rows, part_rows), BF16))(gate, *early)
    other_taps = cross(own_taps, "rep")
    transform_scratch = [block_scratch, stage_scratch] + half_pair
    input_spec = call(signal_kernel, spec_shape, transform_scratch, 6 * 10**6)(
        *early, first, turn, small, forward
    )
    grad_spec, mine, theirs = call(
        filter_kernel,
        (spec_shape,) + halves,
        [block_scratch, stage_scratch] + half_pair + [spec_scratch] + back_one + [flat],
        12 * 10**6,
    )(*late, input_spec, first, last, turn, small, forward, inverse)
    mine_other = cross(mine, "rep")
    near = swap(theirs)
    near_other = cross(near, "rep")
    taps_spec = call(taps_spec_kernel, spec_shape, transform_scratch, 6 * 10**6)(
        own_taps, other_taps, first, turn, small, forward
    )
    input_sent = call(
        input_kernel, pieces(tok_rows), [spec_scratch] + back_one + [flat], 6 * 10**6
    )(grad_spec, taps_spec, last, turn, small, inverse)
    input_back = exchange(input_sent)
    input_back += tuple(swap(piece) for piece in input_back)
    filter_back = exchange(call(sum_kernel, pieces(tok_rows))(mine, mine_other, near, near_other))
    grad_input = call(final_kernel, shape((tok_rows, chan_width), BF16), [block_scratch])(*input_back)
    grad_filter = call(final_kernel, shape((tok_rows, chan_width), F32), [block_scratch])(*filter_back)
    return grad_input.reshape(1, tok_rows, chan_width), grad_filter


def solution(mesh):
    few = mesh.shape["seq"] == CORES * MAX_DIRECT
    body = per_device_near if few else per_device_wide

    return jax.shard_map(
        body,
        mesh=mesh,
        in_specs=(
            P("rep", "seq", "chan"),
            P("rep", "seq", "chan"),
            P("seq", "chan"),
            P("chan", None),
        ),
        out_specs=(P("rep", "seq", "chan"), P("seq", "chan")),
        check_vma=False,
    )
```

```python
import math

import jax
import jax.numpy as jnp
import numpy as np
from jax import lax
from jax.experimental import pallas as pl
from jax.experimental.pallas import tpu as pltpu
from jax.sharding import PartitionSpec as P


LANES = 128
F32 = jnp.float32
BF16 = jnp.bfloat16
VMEM_LIMIT = 48 * 1024 * 1024
CORES = 2
MAX_DIRECT = 4


def split(values):
    high = values.astype(BF16)
    low = (values - high.astype(F32)).astype(BF16)
    return high, low


def split_table(table):
    table = np.asarray(table, np.float32)
    high = table.astype(BF16)
    low = (table - high.astype(np.float32)).astype(BF16)
    return np.stack([high, low])


def phase(numerator, modulus):
    angle = 2.0 * math.pi * np.mod(numerator, modulus) / modulus
    return np.cos(angle), np.sin(angle)


def tables(devices, groups, narrow, tok_rows):
    length = devices * tok_rows
    tiles = tok_rows // LANES
    rows = groups * devices * narrow
    dev = np.arange(devices)
    quarter = 4 * dev + 1
    cos_d, sin_d = phase(quarter[:, None] * dev[None, :], 4 * devices)
    eye_g, eye_c = np.eye(groups), np.eye(narrow)

    def expand(square):
        return np.einsum("gh,jd,ce->gjchde", eye_g, square, eye_c).reshape(rows, rows)

    cos_d, sin_d = expand(cos_d), expand(sin_d)
    first = split_table(np.concatenate([cos_d, -sin_d], axis=0))
    last = split_table(np.concatenate([cos_d.T, -sin_d.T], axis=1) / length)
    local = np.arange(tok_rows)
    cos_r, sin_r = phase(quarter[:, None] * local[None, :], 4 * length)

    def widen(block):
        block = np.broadcast_to(block[None, :, None, :], (groups, devices, narrow, tok_rows))
        return block.reshape(rows, tok_rows)

    turn = np.stack([widen(cos_r), widen(sin_r)]).astype(np.float32)
    lane = np.arange(LANES)
    step = np.arange(tiles)
    cos_s, sin_s = phase(step[:, None] * lane[None, :], tok_rows)
    small = np.stack([cos_s, sin_s]).astype(np.float32)
    cos_b, sin_b = phase(lane[:, None] * lane[None, :], LANES)
    forward = split_table(np.block([[cos_b, -sin_b], [sin_b, cos_b]]))
    inverse = split_table(np.block([[cos_b, sin_b], [-sin_b, cos_b]]))
    return first, last, turn, small, forward, inverse


def butterflies(real_parts, imag_parts, sign):
    size = len(real_parts)
    if size == 1:
        return real_parts, imag_parts
    even_re, even_im = butterflies(real_parts[0::2], imag_parts[0::2], sign)
    odd_re, odd_im = butterflies(real_parts[1::2], imag_parts[1::2], sign)
    low_re, low_im, high_re, high_im = [], [], [], []
    for index in range(size // 2):
        re, im = odd_re[index], odd_im[index]
        if index == 0:
            turned = (re, im)
        elif 4 * index == size:
            turned = (-im, re) if sign > 0 else (im, -re)
        else:
            angle = sign * 2.0 * math.pi * index / size
            c, s = math.cos(angle), math.sin(angle)
            if 8 * index == size:
                turned = ((re - im) * c, (re + im) * c) if sign > 0 else ((re + im) * c, (im - re) * c)
            else:
                turned = (re * c - im * s, re * s + im * c)
        low_re.append(even_re[index] + turned[0])
        low_im.append(even_im[index] + turned[1])
        high_re.append(even_re[index] - turned[0])
        high_im.append(even_im[index] - turned[1])
    return low_re + high_re, low_im + high_im


def dot(lhs, rhs):
    return jnp.dot(lhs, rhs, preferred_element_type=F32)


CHUNK = 8
GROUP = 32


def spread(block, first, stage):
    table = jnp.concatenate([first[0], first[1]], axis=1)
    stage[...] = dot(table, jnp.concatenate([block, block], axis=0))


def forward_group(group, turn, small, forward, stage, high, low, rows, tiles):
    for start in range(group * GROUP, (group + 1) * GROUP, CHUNK):
        own = slice(start, start + CHUNK)
        res, ims = [], []
        for tile in range(tiles):
            lanes = slice(tile * LANES, (tile + 1) * LANES)
            re = stage[own, lanes]
            im = stage[rows + start : rows + start + CHUNK, lanes]
            c, s = turn[0, own, lanes], turn[1, own, lanes]
            res.append(re * c + im * s)
            ims.append(im * c - re * s)
        res, ims = butterflies(res, ims, -1.0)
        for tile in range(tiles):
            re, im = res[tile], ims[tile]
            if tile > 0:
                c, s = small[0, tile : tile + 1, :], small[1, tile : tile + 1, :]
                re, im = re * c + im * s, im * c - re * s
            at = group * tiles * GROUP + tile * GROUP + start % GROUP
            for part, lane in ((re, 0), (im, LANES)):
                part_high, part_low = split(part)
                high[at : at + CHUNK, lane : lane + LANES] = part_high
                low[at : at + CHUNK, lane : lane + LANES] = part_low
    at = slice(group * tiles * GROUP, (group + 1) * tiles * GROUP)
    return dot(
        jnp.concatenate([high[at, :], low[at, :], high[at, :]], axis=1),
        jnp.concatenate([forward[0], forward[0], forward[1]], axis=0),
    )


def transform(block, first, turn, small, forward, stage, high, low, spectrum, rows):
    tiles = block.shape[1] // LANES
    spread(block, first, stage)
    for group in range(rows // GROUP):
        at = slice(group * tiles * GROUP, (group + 1) * tiles * GROUP)
        spectrum[at, :] = forward_group(group, turn, small, forward, stage, high, low, rows, tiles)


def correlate(value, other):
    vr, vi = value[:, :LANES], value[:, LANES:]
    wr, wi = other[:, :LANES], other[:, LANES:]
    return jnp.concatenate([(vr * wr + vi * wi).astype(BF16), (vi * wr - vr * wi).astype(BF16)], axis=1)


def inverse_group(group, product, turn, small, inverse, back, gathered, rows, tiles):
    at = slice(group * tiles * GROUP, (group + 1) * tiles * GROUP)
    back[at, :] = dot(
        jnp.concatenate([product, product], axis=1),
        jnp.concatenate([inverse[0], inverse[1]], axis=0),
    )
    for start in range(group * GROUP, (group + 1) * GROUP, CHUNK):
        own = slice(start, start + CHUNK)
        res, ims = [], []
        for tile in range(tiles):
            row = group * tiles * GROUP + tile * GROUP + start % GROUP
            re = back[row : row + CHUNK, :LANES]
            im = back[row : row + CHUNK, LANES:]
            if tile > 0:
                c, s = small[0, tile : tile + 1, :], small[1, tile : tile + 1, :]
                re, im = re * c - im * s, im * c + re * s
            res.append(re)
            ims.append(im)
        res, ims = butterflies(res, ims, 1.0)
        for tile in range(tiles):
            lanes = slice(tile * LANES, (tile + 1) * LANES)
            c, s = turn[0, own, lanes], turn[1, own, lanes]
            re, im = res[tile], ims[tile]
            gathered[own, lanes] = (re * c - im * s).astype(BF16)
            gathered[rows + start : rows + start + CHUNK, lanes] = (im * c + re * s).astype(BF16)


def collapse(last, gathered):
    rows = last.shape[1]
    both = dot(jnp.concatenate([last[0], last[1]], axis=0), gathered[...])
    return both[:rows] + both[rows:]


def identity(size, dtype):
    row = lax.broadcasted_iota(jnp.int32, (size, size), 0)
    col = lax.broadcasted_iota(jnp.int32, (size, size), 1)
    return (row == col).astype(dtype)


def flipped(left, right):
    return lax.dot_general(left, right, (((1,), (1,)), ((), ())), preferred_element_type=F32)


def per_device_wide(inputs, cotangent, filter_taps, out_proj):
    devices = lax.axis_size("seq")
    groups = lax.axis_size("rep")
    chans = lax.axis_size("chan")
    tok_rows, chan_width = inputs.shape[1:]
    tiles = tok_rows // LANES
    narrow = chan_width // devices
    rows = chan_width
    first, last, turn, small, forward, inverse = (
        jnp.asarray(t) for t in tables(devices, 1, narrow, tok_rows)
    )
    shape = jax.ShapeDtypeStruct

    def call(kernel, out_shape, scratch=(), cost=3 * 10**6):
        return pl.pallas_call(
            kernel,
            out_shape=out_shape,
            scratch_shapes=scratch,
            compiler_params=pltpu.CompilerParams(vmem_limit_bytes=VMEM_LIMIT),
            cost_estimate=pl.CostEstimate(flops=10**8, bytes_accessed=cost, transcendentals=0),
        )

    def pieces(width):
        return (shape((devices, narrow, width), BF16),)

    def put(out_refs, source, lanes):
        out_refs[0][:, :, lanes] = source[...].reshape(devices, narrow, tok_rows).astype(BF16)

    def take(in_refs, lanes, block):
        block[...] = in_refs[0][:, :, lanes].astype(F32).reshape(rows, tok_rows).astype(BF16)

    def exchange(sent):
        return (lax.all_to_all(sent[0], "seq", split_axis=0, concat_axis=0, tiled=True),)

    count = 1
    front, behind = pl.ds(0, tok_rows), pl.ds(tok_rows, tok_rows)
    flat = pltpu.VMEM((rows, tok_rows), F32)
    block_scratch = pltpu.VMEM((rows, tok_rows), BF16)
    half_pair = [
        pltpu.VMEM((tiles * rows, 2 * LANES), BF16),
        pltpu.VMEM((tiles * rows, 2 * LANES), BF16),
    ]
    back_one = [pltpu.VMEM((2 * rows, tok_rows), BF16)]
    stage_scratch = pltpu.VMEM((2 * rows, tok_rows), F32)
    spec_shape = shape((tiles * rows, 2 * LANES), F32)
    spec_scratch = pltpu.VMEM((tiles * rows, 2 * LANES), F32)

    def pack_kernel(input_ref, taps_ref, *refs):
        *out_refs, wide = refs
        eye = identity(chan_width, BF16)
        wide[...] = flipped(eye, input_ref[...])
        put(out_refs, wide, front)
        wide[...] = flipped(eye, taps_ref[...])
        put(out_refs, wide, behind)

    def mix_kernel(own_ref, other_ref, proj_ref, *refs):
        *out_refs, wide = refs
        chan = lax.axis_index("chan")
        own = pl.ds(pl.multiple_of(chan * chan_width, chan_width), chan_width)
        other = pl.ds(pl.multiple_of((1 - chan) * chan_width, chan_width), chan_width)
        wide[...] = flipped(proj_ref[:, own], own_ref[...]) + flipped(proj_ref[:, other], other_ref[...])
        put(out_refs, wide, front)

    def early_kernel(*refs):
        recv, (first, turn, small, forward, input_ref, taps_ref, block, stage, high, low) = (
            refs[:count], refs[count:],
        )
        for lanes, spectrum in ((front, input_ref), (behind, taps_ref)):
            take(recv, lanes, block)
            transform(block[...], first, turn, small, forward, stage, high, low, spectrum, rows)

    count_groups = rows // GROUP

    def span(group):
        return slice(group * tiles * GROUP, (group + 1) * tiles * GROUP)

    def filter_kernel(*refs):
        recv, rest = refs[:count], refs[count:]
        (input_ref, first, last, turn, small, forward, inverse, grad, out_ref,
         block, stage, high, low, back, back_high) = rest
        take(recv, front, block)
        spread(block[...], first, stage)
        for group in range(count_groups):
            value = forward_group(group, turn, small, forward, stage, high, low, rows, tiles)
            grad[span(group), :] = value
            product = correlate(value, input_ref[span(group), :])
            inverse_group(group, product, turn, small, inverse, back, back_high, rows, tiles)
        out_ref[...] = collapse(last, back_high).astype(BF16)

    def input_kernel(grad, taps_ref, last, turn, small, inverse, *refs):
        *out_refs, back, back_high, wide = refs
        for group in range(count_groups):
            product = correlate(grad[span(group), :], taps_ref[span(group), :])
            inverse_group(group, product, turn, small, inverse, back, back_high, rows, tiles)
        wide[...] = collapse(last, back_high)
        put(out_refs, wide, front)

    def sum_kernel(own_ref, other_ref, *refs):
        *out_refs, wide = refs
        wide[...] = own_ref[...].astype(F32) + other_ref[...].astype(F32)
        put(out_refs, wide, front)

    def final_kernel(*refs):
        *recv, out_ref, block = refs
        take(recv, front, block)
        moved = lax.dot_general(
            block[...], identity(chan_width, BF16), (((0,), (0,)), ((), ())), preferred_element_type=F32
        )
        out_ref[...] = moved.astype(out_ref.dtype)

    own = cotangent.reshape(tok_rows, chan_width)
    other = lax.ppermute(own, "chan", [(k, (k + 1) % chans) for k in range(chans)])
    early = exchange(
        call(pack_kernel, pieces(2 * tok_rows), [flat])(inputs.reshape(tok_rows, chan_width), filter_taps)
    )
    late = exchange(call(mix_kernel, pieces(tok_rows), [flat])(own, other, out_proj))
    input_spec, taps_spec = call(
        early_kernel, (spec_shape, spec_shape), [block_scratch, stage_scratch] + half_pair, 9 * 10**6
    )(*early, first, turn, small, forward)
    grad_spec, partial = call(
        filter_kernel,
        (spec_shape, shape((rows, tok_rows), BF16)),
        [block_scratch, stage_scratch] + half_pair + [spec_scratch] + back_one,
        9 * 10**6,
    )(*late, input_spec, first, last, turn, small, forward, inverse)
    partial_other = lax.ppermute(partial, "rep", [(k, (k + 1) % groups) for k in range(groups)])
    input_back = exchange(
        call(input_kernel, pieces(tok_rows), [spec_scratch] + back_one + [flat], 6 * 10**6)(
            grad_spec, taps_spec, last, turn, small, inverse
        )
    )
    filter_back = exchange(call(sum_kernel, pieces(tok_rows), [flat])(partial, partial_other))
    grad_input = call(final_kernel, shape((tok_rows, chan_width), BF16), [block_scratch])(*input_back)
    grad_filter = call(final_kernel, shape((tok_rows, chan_width), F32), [block_scratch])(*filter_back)
    return grad_input.reshape(1, tok_rows, chan_width), grad_filter


def per_device_near(inputs, cotangent, filter_taps, out_proj):
    devices = lax.axis_size("seq")
    groups = lax.axis_size("rep")
    tok_rows, chan_width = inputs.shape[1:]
    tiles = tok_rows // LANES
    narrow = chan_width // devices
    rows = chan_width
    chips = devices // CORES
    wide_rows = CORES * narrow
    half = chips * narrow
    first, last, turn, small, forward, inverse = (
        jnp.asarray(t) for t in tables(devices, 1, narrow, tok_rows)
    )
    shape = jax.ShapeDtypeStruct
    swap_pairs = [(k, k ^ 1) for k in range(devices)]

    def call(kernel, out_shape, scratch=(), cost=3 * 10**6):
        return pl.pallas_call(
            kernel,
            out_shape=out_shape,
            scratch_shapes=scratch,
            compiler_params=pltpu.CompilerParams(vmem_limit_bytes=VMEM_LIMIT),
            cost_estimate=pl.CostEstimate(flops=10**8, bytes_accessed=cost, transcendentals=0),
        )

    def swap(value):
        return lax.ppermute(value, "seq", swap_pairs)

    def cross(value, axis):
        size = lax.axis_size(axis)
        return lax.ppermute(value, axis, [(k, (k + 1) % size) for k in range(size)])

    def exchange(sent):
        got = [sent[0]]
        for offset in range(1, chips):
            pairs = [(k, k ^ (offset * CORES)) for k in range(devices)]
            got.append(lax.ppermute(sent[offset], "seq", pairs))
        return tuple(got)

    def place():
        at = lax.axis_index("seq")
        return at // CORES, at % CORES

    def pieces(width):
        return tuple(shape((CORES, narrow, width), BF16) for _ in range(chips))

    part_rows = tok_rows // groups
    front, behind = pl.ds(0, tok_rows), pl.ds(tok_rows, part_rows)
    block_scratch = pltpu.VMEM((rows, tok_rows), BF16)
    half_pair = [
        pltpu.VMEM((tiles * rows, 2 * LANES), BF16),
        pltpu.VMEM((tiles * rows, 2 * LANES), BF16),
    ]
    back_one = [pltpu.VMEM((2 * rows, tok_rows), BF16)]
    stage_scratch = pltpu.VMEM((2 * rows, tok_rows), F32)
    spec_shape = shape((tiles * rows, 2 * LANES), F32)
    spec_scratch = pltpu.VMEM((tiles * rows, 2 * LANES), F32)
    flat = pltpu.VMEM((rows, tok_rows), F32)
    half_scratch = pltpu.VMEM((half, tok_rows), F32)
    halves = (shape((chips, narrow, tok_rows), BF16), shape((chips, narrow, tok_rows), BF16))

    def put(out_refs, source, side, lanes, part=slice(None)):
        chip, _ = place()
        for offset in range(chips):
            at = pl.multiple_of((chip ^ offset) * narrow, narrow)
            out_refs[offset][pl.ds(side, 1), :, lanes] = (
                source[pl.ds(at, narrow), part][None].astype(BF16)
            )

    def take(in_refs, lanes, block):
        chip, _ = place()
        for offset in range(chips):
            at = pl.multiple_of((chip ^ offset) * wide_rows, wide_rows)
            for core in range(CORES):
                block[pl.ds(at + core * narrow, narrow), :] = in_refs[offset][core, :, lanes]

    def cut(source, mine_ref, theirs_ref):
        _, core = place()
        for chip in range(chips):
            for ref, side in ((mine_ref, core), (theirs_ref, 1 - core)):
                at = pl.multiple_of(chip * wide_rows + side * narrow, narrow)
                ref[chip] = source[pl.ds(at, narrow), :].astype(BF16)

    def chosen(core):
        row = lax.broadcasted_iota(jnp.int32, (half, chan_width), 0)
        col = lax.broadcasted_iota(jnp.int32, (half, chan_width), 1)
        pick = (row // narrow) * wide_rows + core * narrow + row % narrow
        return (pick == col).astype(F32).astype(BF16)

    def pack_kernel(input_ref, taps_ref, input_near, taps_near, *refs):
        *out_refs, wide = refs
        _, core = place()
        pick = chosen(core)
        part = pl.ds(0, part_rows)
        for own_ref, near_ref, lanes, span_in in (
            (input_ref, input_near, front, slice(None)), (taps_ref, taps_near, behind, part),
        ):
            for ref, side in ((own_ref, core), (near_ref, 1 - core)):
                wide[:, span_in] = flipped(pick, ref[...])
                put(out_refs, wide, side, lanes, span_in)

    def taps_kernel(gate_ref, *refs):
        *recv, out_ref = refs
        take(recv, behind, out_ref)

    def own_kernel(own_ref, proj_ref, near_ref, part_ref, part_near, other_ref):
        chan = lax.axis_index("chan")
        _, core = place()
        picked = [
            proj_ref[pl.ds(pl.multiple_of(chip * wide_rows + core * narrow, narrow), narrow), :]
            for chip in range(chips)
        ]
        held = jnp.concatenate(picked, axis=0)
        swapped = jnp.concatenate([held[:, chan_width:], held[:, :chan_width]], axis=1)
        held = jnp.where(chan == 0, held, swapped)
        part_ref[...] = flipped(held[:, :chan_width], own_ref[...])
        part_near[...] = flipped(held[:, :chan_width], near_ref[...])
        other_ref[...] = held[:, chan_width:]

    def mix_kernel(part_ref, part_near, proj_ref, other_ref, other_near, *refs):
        *out_refs, wide = refs
        _, core = place()
        for part, ref, side in ((part_ref, other_ref, core), (part_near, other_near, 1 - core)):
            wide[...] = part[...] + flipped(proj_ref[...], ref[...])
            put(out_refs, wide, side, front)

    def signal_kernel(*refs):
        recv, (first, turn, small, forward, spectrum, block, stage, high, low) = refs[:chips], refs[chips:]
        take(recv, front, block)
        transform(block[...], first, turn, small, forward, stage, high, low, spectrum, rows)

    def taps_spec_kernel(own_ref, other_ref, first, turn, small, forward, spectrum, block, stage, high, low):
        index = lax.axis_index("rep")
        for ref, at in ((own_ref, index), (other_ref, 1 - index)):
            block[:, pl.ds(pl.multiple_of(at * part_rows, part_rows), part_rows)] = ref[...]
        transform(block[...], first, turn, small, forward, stage, high, low, spectrum, rows)

    count_groups = rows // GROUP

    def span(group):
        return slice(group * tiles * GROUP, (group + 1) * tiles * GROUP)

    def filter_kernel(grad, input_ref, last, turn, small, inverse, mine_ref, theirs_ref, back, back_high, wide):
        for group in range(count_groups):
            product = correlate(grad[span(group), :], input_ref[span(group), :])
            inverse_group(group, product, turn, small, inverse, back, back_high, rows, tiles)
        wide[...] = collapse(last, back_high)
        cut(wide, mine_ref, theirs_ref)

    def input_kernel(grad, taps_ref, last, turn, small, inverse, *refs):
        *out_refs, back, back_high, wide = refs
        for group in range(count_groups):
            product = correlate(grad[span(group), :], taps_ref[span(group), :])
            inverse_group(group, product, turn, small, inverse, back, back_high, rows, tiles)
        wide[...] = collapse(last, back_high)
        chip, _ = place()
        for offset in range(chips):
            at = pl.multiple_of((chip ^ offset) * wide_rows, wide_rows)
            out_refs[offset][...] = (
                wide[pl.ds(at, wide_rows), :].reshape(CORES, narrow, tok_rows).astype(BF16)
            )

    def gate_kernel(value_ref, out_ref):
        out_ref[...] = value_ref[:16, :]

    def sum_kernel(mine_ref, mine_other, near_ref, near_other, *out_refs):
        chip, core = place()
        for offset in range(chips):
            at = pl.ds(chip ^ offset, 1)
            for ref, other, side in ((mine_ref, mine_other, core), (near_ref, near_other, 1 - core)):
                total = ref[at].astype(F32) + other[at].astype(F32)
                out_refs[offset][pl.ds(side, 1)] = total.astype(BF16)

    def final_kernel(*refs):
        *recv, out_ref, block = refs
        if len(recv) == chips:
            take(recv, front, block)
        else:
            chip, core = place()
            for offset in range(chips):
                for flip in range(CORES):
                    at = pl.multiple_of((chip ^ offset) * wide_rows + (core ^ flip) * narrow, narrow)
                    block[pl.ds(at, narrow), :] = recv[flip * chips + offset][core]
        moved = lax.dot_general(
            block[...], identity(chan_width, BF16), (((0,), (0,)), ((), ())), preferred_element_type=F32
        )
        out_ref[...] = moved.astype(out_ref.dtype)

    signal = inputs.reshape(tok_rows, chan_width)
    own = cotangent.reshape(tok_rows, chan_width)
    signal_near = swap(signal)
    taps_part = lax.dynamic_slice_in_dim(filter_taps, lax.axis_index("rep") * part_rows, part_rows, 0)
    taps_near = swap(taps_part)
    other = cross(own, "chan")
    own_near = swap(own)
    early = exchange(
        call(
            pack_kernel,
            pieces(tok_rows + part_rows),
            [half_scratch],
        )(signal, taps_part, signal_near, taps_near),
    )
    part_shape = shape((half, tok_rows), F32)
    part, part_near, proj_other = call(
        own_kernel,
        (part_shape, part_shape, shape((half, chan_width), BF16)),
    )(own, out_proj, own_near)
    other_near = swap(other)
    late = exchange(call(mix_kernel, pieces(tok_rows), [half_scratch])(part, part_near, proj_other, other, other_near))
    gate = call(gate_kernel, shape((16, chan_width), BF16), (), 10**4)(proj_other)
    own_taps = call(taps_kernel, shape((rows, part_rows), BF16))(gate, *early)
    other_taps = cross(own_taps, "rep")
    transform_scratch = [block_scratch, stage_scratch] + half_pair
    input_spec = call(signal_kernel, spec_shape, transform_scratch, 6 * 10**6)(
        *early, first, turn, small, forward
    )
    grad_spec = call(signal_kernel, spec_shape, transform_scratch, 6 * 10**6)(
        *late, first, turn, small, forward
    )
    mine, theirs = call(
        filter_kernel, halves, [spec_scratch] + back_one + [flat], 6 * 10**6
    )(grad_spec, input_spec, last, turn, small, inverse)
    mine_other = cross(mine, "rep")
    near = swap(theirs)
    near_other = cross(near, "rep")
    taps_spec = call(taps_spec_kernel, spec_shape, transform_scratch, 6 * 10**6)(
        own_taps, other_taps, first, turn, small, forward
    )
    input_sent = call(
        input_kernel, pieces(tok_rows), [spec_scratch] + back_one + [flat], 6 * 10**6
    )(grad_spec, taps_spec, last, turn, small, inverse)
    input_back = exchange(input_sent)
    input_back += tuple(swap(piece) for piece in input_back)
    filter_back = exchange(call(sum_kernel, pieces(tok_rows))(mine, mine_other, near, near_other))
    grad_input = call(final_kernel, shape((tok_rows, chan_width), BF16), [block_scratch])(*input_back)
    grad_filter = call(final_kernel, shape((tok_rows, chan_width), F32), [block_scratch])(*filter_back)
    return grad_input.reshape(1, tok_rows, chan_width), grad_filter


def solution(mesh):
    few = mesh.shape["seq"] == CORES * MAX_DIRECT
    body = per_device_near if few else per_device_wide

    return jax.shard_map(
        body,
        mesh=mesh,
        in_specs=(
            P("rep", "seq", "chan"),
            P("rep", "seq", "chan"),
            P("seq", "chan"),
            P("chan", None),
        ),
        out_specs=(P("rep", "seq", "chan"), P("seq", "chan")),
        check_vma=False,
    )
```
